256 devices in a mesh: batch: 4 (over x_lo, core), seq: 64 (over y, z, x_hi).
Axes of the slice: x: 4 (x_hi: 2, x_lo: 2; x = x_hi * 2 + x_lo), y: 4, z: 8, core: 2. Of those that a mesh axis runs over, the one named last changes fastest.
Arguments:
- tokens: bfloat16 [1216, 262144], P('batch', 'seq'), parts along dimension 0, may hold values from -6 to 6
- norm_gain: float32 [2, 304], replicated, may hold values from 0.5 to 1.5
- in_weight: bfloat16 [2, 608, 304], replicated, may hold values from -0.3125 to 0.3125
- in_bias: float32 [2, 608], replicated, may hold values from -3 to 3
- out_weight: bfloat16 [2, 304, 608], replicated, may hold values from -0.25 to 0.25
- out_bias: float32 [2, 304], replicated, may hold values from -3 to 3
Outputs:
- mixed: bfloat16 [1216, 262144], P('batch', 'seq'), parts along dimension 0
The draws below stay inside these ranges and needn't reach their ends.
There are 4 independent parts, one for each index of `batch`. The reference program is written for one: setup_inputs(seed, part) draws one part's arguments, and reference() takes and returns one part's arrays. A program takes and returns all parts, laid end to end along the dimension named above; an argument that names none is the same for every part. Nothing has to cross between parts.
All inputs are finite; a program needn't handle non-finite values.
Results may differ from the reference program's by a relative error of at most 0.0056.
Values may be sent and summed in bfloat16 or wider, within the bound.
No kernel may reach another device: no remote copies, remote signals or barrier semaphores. Data moves between devices by JAX's collectives and lax.ppermute only.
A program may use at most 64 MiB of HBM per device.

```python
import jax
import jax.numpy as jnp
from jax import lax

TRACK_CH = 16
TRACKS = 19
LENGTH = 262144
BLOCKS = 2
D = 304
HID = 608


def shard_levels(key, extent, split, smallest, largest):
    loudness, own = 1.0, jax.random.fold_in(key, 6)
    for axis_at, shards_of in split:
        heights = jnp.exp(jax.random.uniform(jax.random.fold_in(own, axis_at), (shards_of,), jnp.float32, smallest / len(split), largest / len(split)))
        loudness = loudness * jnp.repeat(heights, extent[axis_at] // shards_of).reshape([-1 if axis == axis_at else 1 for axis in range(len(extent))])
    return loudness


def normal_values(stream_key, extent, deviation, bound, split=(), kind=jnp.bfloat16):
    array = deviation * jax.random.normal(stream_key, extent, jnp.float32)
    if split:
        array = array * shard_levels(stream_key, extent, split, -0.22, 0.18)
    return jnp.clip(array, -bound, bound).astype(kind)


def setup_inputs(seed: int = 0, part: int = 0) -> dict:
    seeds = jax.random.split(jax.random.key(seed), 7)
    part_keys = jax.random.split(jax.random.fold_in(seeds[6], part), 7)
    tokens = normal_values(part_keys[0], (D, LENGTH), 1.0, 6.0, ((1, 64),))
    norm_gain = jnp.clip(jax.random.uniform(seeds[1], (BLOCKS, D), jnp.float32, 0.5, 1.5), 0.5, 1.5)
    in_weight = normal_values(seeds[2], (BLOCKS, HID, D), D ** -0.5, 0.3125)
    in_bias = normal_values(seeds[3], (BLOCKS, HID), 0.5, 3.0, (), jnp.float32)
    out_weight = normal_values(seeds[4], (BLOCKS, D, HID), HID ** -0.5, 0.25)
    out_bias = normal_values(seeds[5], (BLOCKS, D), 0.5, 3.0, (), jnp.float32)
    return dict(tokens=tokens, norm_gain=norm_gain, in_weight=in_weight, in_bias=in_bias, out_weight=out_weight, out_bias=out_bias)


def rotate(current):
    pieces = [current[0:TRACK_CH]]
    for track_no in range(1, TRACKS):
        offset = 2 ** (track_no - 1)
        one_track = current[track_no * TRACK_CH:(track_no + 1) * TRACK_CH]
        pieces.append(jnp.roll(one_track, offset, axis=1))
    return jnp.concatenate(pieces, 0)

def mix_rows(rotated, gain, in_weight, in_bias, out_weight, out_bias):
    as_float = rotated.astype(jnp.float32)
    mean_square = lax.optimization_barrier(jnp.mean(as_float * as_float, axis=0, keepdims=True))
    normed = (as_float * gain[:, None] * lax.rsqrt(mean_square + 1e-06)).astype(jnp.bfloat16)
    pre_act = jnp.dot(in_weight, normed, preferred_element_type=jnp.float32) + in_bias[:, None]
    active = jax.nn.gelu(pre_act, approximate=True).astype(jnp.bfloat16)
    summed = as_float + jnp.dot(out_weight, active, preferred_element_type=jnp.float32) + out_bias[:, None]
    return summed.astype(jnp.bfloat16)

def reference(tokens, norm_gain, in_weight, in_bias, out_weight, out_bias):
    current = tokens
    piece_count = 64
    piece_cols = LENGTH // piece_count
    for block_no in range(BLOCKS):
        rotated = rotate(current)
        stacked = rotated.reshape(D, piece_count, piece_cols).transpose(1, 0, 2)
        result = lax.map(lambda column_block: mix_rows(column_block, norm_gain[block_no], in_weight[block_no], in_bias[block_no], out_weight[block_no], out_bias[block_no]), stacked)
        current = result.transpose(1, 0, 2).reshape(D, LENGTH)
    return current
```

```python
import functools

import jax
import jax.numpy as jnp
from jax import lax
from jax.experimental import pallas as pl
from jax.experimental.pallas import tpu as pltpu
from jax.sharding import PartitionSpec as P

TRACK_CH = 16
TRACKS = 19
BLOCKS = 2
LANES = 128
TILE = 512
GELU_A = 0.7978845608028654
GELU_B = 0.7978845608028654 * 0.044715


def shifted(value, axis, steps):
    count = lax.axis_size(axis)
    pairs = [(source, (source + steps) % count) for source in range(count)]
    return lax.ppermute(value, axis, pairs)


def short_tracks(local_rows):
    count = 0
    while count + 1 < TRACKS and 2**count < local_rows:
        count = count + 1
    return count


def pack_halo(track, store, local_rows, short_count):
    lane = lax.broadcasted_iota(jnp.int32, (TRACK_CH, LANES), 1)
    packed = jnp.zeros((TRACK_CH, LANES), jnp.float32)
    for slot in range(short_count):
        offset = 2**slot
        if offset < LANES:
            last = track(1 + slot, local_rows - LANES, local_rows).astype(jnp.float32)
            moved = pltpu.roll(last, (2 * offset - 1) % LANES, 1)
            inside = (lane >= offset - 1) & (lane < 2 * offset - 1)
            packed = jnp.where(inside, moved, packed)
        else:
            store(offset, 2 * offset, track(1 + slot, local_rows - offset, local_rows))
    store(0, LANES, packed.astype(jnp.bfloat16))


def rotated_piece(track, halo, slot, begin, end):
    offset = 2**slot
    if offset < LANES:
        if begin == 0:
            packed = halo(0, LANES).astype(jnp.float32)
            before = pltpu.roll(packed, (LANES + 1 - 2 * offset) % LANES, 1)
            window = jnp.concatenate([before, track(1 + slot, 0, end).astype(jnp.float32)], 1)
        else:
            window = track(1 + slot, begin - LANES, end).astype(jnp.float32)
        return pltpu.roll(window, offset, 1)[:, LANES:]
    parts = []
    if begin < offset:
        parts.append(halo(offset + begin, offset + min(end, offset)))
    if end > offset:
        parts.append(track(1 + slot, max(begin, offset) - offset, end - offset))
    joined = parts[0] if len(parts) == 1 else jnp.concatenate(parts, 1)
    return joined.astype(jnp.float32)


def mix(rotated, gain, w_in, b_in, w_out, b_out):
    mean_square = jnp.mean(rotated * rotated, axis=0, keepdims=True)
    normed = (rotated * gain * lax.rsqrt(mean_square + 1e-06)).astype(jnp.bfloat16)
    pre = jnp.dot(w_in, normed, preferred_element_type=jnp.float32) + b_in
    inner = pre * (GELU_A + GELU_B * (pre * pre))
    half = 0.5 * pre
    active = (half + half * jnp.tanh(inner)).astype(jnp.bfloat16)
    out = jnp.dot(w_out, active, preferred_element_type=jnp.float32)
    return (rotated + out + b_out).astype(jnp.bfloat16)


def halo_kernel(local_rows, short_count, tail, out):
    base = local_rows - tail.shape[1]

    def track(t, begin, end):
        return tail[t * TRACK_CH : (t + 1) * TRACK_CH, begin - base : end - base]

    def store(begin, end, value):
        out[:, begin:end] = value

    pack_halo(track, store, local_rows, short_count)


def block_kernel(short_count, last, *refs):
    far_count = TRACKS - 1 - short_count
    near, halo_in = refs[0], refs[1]
    far = refs[2 : 2 + far_count]
    gain, w_in, b_in, w_out, b_out = refs[2 + far_count : 7 + far_count]
    outs = refs[7 + far_count :]
    local_rows = halo_in.shape[1]
    near_rows = (1 + short_count) * TRACK_CH

    def track(t, begin, end):
        return near[t * TRACK_CH : (t + 1) * TRACK_CH, begin:end]

    def halo(begin, end):
        return halo_in[:, begin:end]

    for begin in range(0, local_rows, TILE):
        end = begin + TILE
        pieces = [track(0, begin, end).astype(jnp.float32)]
        for slot in range(short_count):
            pieces.append(rotated_piece(track, halo, slot, begin, end))
        for ref in far:
            pieces.append(ref[:, begin:end].astype(jnp.float32))
        rotated = jnp.concatenate(pieces, 0)
        mixed = mix(rotated, gain[...], w_in[...], b_in[...], w_out[...], b_out[...])
        if last:
            outs[0][:, begin:end] = mixed
        else:
            outs[0][:, begin:end] = mixed[:near_rows]
            for at in range(far_count):
                top = near_rows + at * TRACK_CH
                outs[2 + at][:, begin:end] = mixed[top : top + TRACK_CH]
    if not last:

        def made(t, begin, end):
            return outs[0][t * TRACK_CH : (t + 1) * TRACK_CH, begin:end]

        def store(begin, end, value):
            outs[1][:, begin:end] = value

        pack_halo(made, store, local_rows, short_count)


VMEM = pl.BlockSpec(memory_space=pltpu.VMEM)


def shards(tokens, norm_gain, in_weight, in_bias, out_weight, out_bias):
    width, local_rows = tokens.shape
    short_count = short_tracks(local_rows)
    far_count = TRACKS - 1 - short_count
    near_rows = (1 + short_count) * TRACK_CH
    one = jax.ShapeDtypeStruct((TRACK_CH, local_rows), jnp.bfloat16)
    near = tokens[:near_rows]
    bundle = pl.pallas_call(
        functools.partial(halo_kernel, local_rows, short_count),
        out_shape=one,
        grid=(1,),
        in_specs=[pl.BlockSpec((near_rows, local_rows // 2), lambda i: (0, 1))],
        out_specs=pl.BlockSpec((TRACK_CH, local_rows), lambda i: (0, 0)),
        name="halo",
    )(tokens)
    far = [tokens[near_rows + at * TRACK_CH : near_rows + (at + 1) * TRACK_CH] for at in range(far_count)]
    for block_no in range(BLOCKS):
        last = block_no == BLOCKS - 1
        halo = shifted(bundle, "seq", 1)
        far = [
            shifted(value, "seq", 2 ** (short_count + at) // local_rows)
            for at, value in enumerate(far)
        ]
        if last:
            out_shape = [jax.ShapeDtypeStruct((width, local_rows), jnp.bfloat16)]
        else:
            out_shape = [jax.ShapeDtypeStruct((near_rows, local_rows), jnp.bfloat16)] + [one] * (1 + far_count)
        outs = pl.pallas_call(
            functools.partial(block_kernel, short_count, last),
            out_shape=out_shape,
            in_specs=[VMEM] * (7 + far_count),
            out_specs=[VMEM] * len(out_shape),
            compiler_params=pltpu.CompilerParams(vmem_limit_bytes=40 << 20),
            name="block",
        )(
            near,
            halo,
            *far,
            norm_gain[block_no][:, None],
            in_weight[block_no],
            in_bias[block_no][:, None],
            out_weight[block_no],
            out_bias[block_no][:, None],
        )
        if last:
            return outs[0]
        near, bundle, far = outs[0], outs[1], outs[2:]


def solution(mesh):
    return jax.shard_map(
        shards,
        mesh=mesh,
        in_specs=(P("batch", "seq"), P(), P(), P(), P(), P()),
        out_specs=P("batch", "seq"),
        check_vma=False,
    )
```

```python
import functools

import jax
import jax.numpy as jnp
from jax import lax
from jax.experimental import pallas as pl
from jax.experimental.pallas import tpu as pltpu
from jax.sharding import PartitionSpec as P

TRACK_CH = 16
TRACKS = 19
BLOCKS = 2
LANES = 128
NEAR_TILE = 1024
FAR_TILE = 1024
OUT_TILE = 1024
COST = 1
LIMITS = 8, 12, 8
GELU_A = 0.7978845608028654
GELU_B = 0.7978845608028654 * 0.044715
F32, BF16 = jnp.float32, jnp.bfloat16
VMEM = pl.BlockSpec(memory_space=pltpu.VMEM)


def shifted(value, axis, steps):
    count = lax.axis_size(axis)
    pairs = [(source, (source + steps) % count) for source in range(count)]
    return lax.ppermute(value, axis, pairs)


def after(value, *others):
    return lax.optimization_barrier((value, *others))[0]


def short_tracks(local_rows):
    count = 0
    while count + 1 < TRACKS and 2**count < local_rows:
        count = count + 1
    return count


def pack_halo(track, store, local_rows, short_count):
    lane = lax.broadcasted_iota(jnp.int32, (TRACK_CH, LANES), 1)
    packed = jnp.zeros((TRACK_CH, LANES), F32)
    for slot in range(short_count):
        offset = 2**slot
        if offset < LANES:
            last = track(1 + slot, local_rows - LANES, local_rows).astype(F32)
            moved = pltpu.roll(last, (2 * offset - 1) % LANES, 1)
            inside = (lane >= offset - 1) & (lane < 2 * offset - 1)
            packed = jnp.where(inside, moved, packed)
        else:
            store(offset, 2 * offset, track(1 + slot, local_rows - offset, local_rows))
    store(0, LANES, packed.astype(BF16))


def rotated_piece(track, halo, slot, begin, end):
    offset = 2**slot
    if offset < LANES:
        if begin == 0:
            packed = halo(0, LANES).astype(F32)
            before = pltpu.roll(packed, (LANES + 1 - 2 * offset) % LANES, 1)
            window = jnp.concatenate([before, track(1 + slot, 0, end).astype(F32)], 1)
        else:
            window = track(1 + slot, begin - LANES, end).astype(F32)
        return pltpu.roll(window, offset, 1)[:, LANES:].astype(BF16)
    parts = []
    if begin < offset:
        parts.append(halo(offset + begin, offset + min(end, offset)))
    if end > offset:
        parts.append(track(1 + slot, max(begin, offset) - offset, end - offset))
    return parts[0] if len(parts) == 1 else jnp.concatenate(parts, 1)


def split_kernel(first_row, tokens, *refs):
    count = len(refs) // 2
    copies = []
    for at in range(count):
        top = first_row + at * TRACK_CH
        copies.append(
            pltpu.make_async_copy(tokens.at[top : top + TRACK_CH, :], refs[at], refs[count + at])
        )
    for copy in copies:
        copy.start()
    for copy in copies:
        copy.wait()


def halo_kernel(local_rows, short_count, tail, out):
    base = local_rows - tail.shape[1]

    def track(t, begin, end):
        return tail[t * TRACK_CH : (t + 1) * TRACK_CH, begin - base : end - base]

    def store(begin, end, value):
        out[:, begin:end] = value

    pack_halo(track, store, local_rows, short_count)


def near_kernel(short_count, first, *refs):
    near, gain, w_in, *halo_in = refs[:-3]
    rotated, squares, partial = refs[-3:]
    near_rows, width = rotated.shape

    def track(t, begin, end):
        return near[t * TRACK_CH : (t + 1) * TRACK_CH, begin:end]

    def halo(begin, end):
        return halo_in[0][:, begin:end]

    for at in range(0, width, NEAR_TILE):
        begin, end = first + at, first + at + NEAR_TILE
        total = jnp.zeros((8, NEAR_TILE), F32)
        scaled = []
        for t in range(1 + short_count):
            rows = slice(t * TRACK_CH, (t + 1) * TRACK_CH)
            piece = track(0, begin, end) if t == 0 else rotated_piece(track, halo, t - 1, begin, end)
            rotated[rows, at : at + NEAR_TILE] = piece
            piece = piece.astype(F32)
            total = total + (piece[:8] * piece[:8] + piece[8:] * piece[8:])
            scaled.append((piece * gain[rows]).astype(BF16))
        squares[:, at : at + NEAR_TILE] = total
        partial[:, at : at + NEAR_TILE] = jnp.dot(
            w_in[:, :near_rows], jnp.concatenate(scaled, 0), preferred_element_type=F32
        ).astype(BF16)


def far_kernel(near_rows, last, *refs):
    nears = refs[:6]
    far = refs[6:12]
    gain, w_in, b_in, w_out, b_out = refs[12:17]
    outs = refs[17:]
    local_rows = far[0].shape[1]
    half_rows = local_rows // 2
    width = near_rows + len(far) * TRACK_CH
    for begin in range(0, local_rows, FAR_TILE):
        end = begin + FAR_TILE
        rotated, squares, partial = nears[:3] if begin < half_rows else nears[3:]
        at = begin % half_rows
        here = slice(at, at + FAR_TILE)
        parts = [ref[:, begin:end].astype(F32) for ref in far]
        total = squares[:, here]
        for part in parts:
            total = total + (part[:8] * part[:8] + part[8:] * part[8:])
        scale = lax.rsqrt(jnp.sum(total, axis=0, keepdims=True) * (1.0 / width) + 1e-06)
        far_part = jnp.concatenate(parts, 0)
        scaled = (far_part * gain[near_rows:]).astype(BF16)
        pre = partial[:, here].astype(F32) + jnp.dot(w_in[:, near_rows:], scaled, preferred_element_type=F32)
        pre = pre * scale + b_in[...]
        inner = pre * (GELU_A + GELU_B * (pre * pre))
        half = 0.5 * pre
        active = (half + half * jnp.tanh(inner)).astype(BF16)
        if last:
            out = jnp.dot(w_out[...], active, preferred_element_type=F32) + b_out[...]
            outs[0][:near_rows, begin:end] = (rotated[:, here].astype(F32) + out[:near_rows]).astype(BF16)
            outs[0][near_rows:, begin:end] = (far_part + out[near_rows:]).astype(BF16)
        else:
            out = jnp.dot(w_out[near_rows:], active, preferred_element_type=F32)
            mixed = (far_part + out + b_out[near_rows:]).astype(BF16)
            outs[0][:, begin:end] = active
            for track in range(len(far)):
                outs[1 + track][:, begin:end] = mixed[track * TRACK_CH : (track + 1) * TRACK_CH]


def out_kernel(short_count, low, high, active, w_out, b_out, near, bundle):
    near_rows, local_rows = near.shape
    half_rows = local_rows // 2
    for begin in range(0, local_rows, OUT_TILE):
        end = begin + OUT_TILE
        rotated = low if begin < half_rows else high
        at = begin % half_rows
        out = jnp.dot(w_out[:near_rows], active[:, begin:end], preferred_element_type=F32)
        kept = rotated[:, at : at + OUT_TILE].astype(F32)
        near[:, begin:end] = (kept + out + b_out[:near_rows]).astype(BF16)

    def track(t, begin, end):
        return near[t * TRACK_CH : (t + 1) * TRACK_CH, begin:end]

    def store(begin, end, value):
        bundle[:, begin:end] = value

    pack_halo(track, store, local_rows, short_count)


def call(kernel, out_shape, count, name, limit):
    return pl.pallas_call(
        kernel,
        out_shape=out_shape,
        in_specs=[VMEM] * count,
        out_specs=[VMEM] * len(out_shape),
        compiler_params=pltpu.CompilerParams(vmem_limit_bytes=limit << 20),
        cost_estimate=pl.CostEstimate(flops=COST, transcendentals=0, bytes_accessed=COST),
        name=name,
    )


def permuted(value, moves):
    return lax.ppermute(value, "seq", moves)


def routes():
    first, second = [], []
    for y in range(4):
        for z in range(8):
            for x in range(2):
                source = (y * 8 + z) * 2 + x
                middle = (((y + z // 4) % 4) * 8 + (z - 2) % 8) * 2 + x
                first.append((source, middle))
                second.append((middle, (source + 8) % 64))
    return first, second


def first_moves(far):
    to_middle, _ = routes()
    eight = permuted(far[3], to_middle)
    one = shifted(far[0], "seq", 1)
    back = shifted(far[5], "seq", -16)
    four = shifted(far[2], "seq", 4)
    two = shifted(far[1], "seq", 2)
    return eight, one, back, four, two


def last_moves(far, firsts, bundle):
    _, from_middle = routes()
    eight, one, back, four, two = firsts
    eight = permuted(eight, from_middle)
    back = shifted(back, "seq", -16)
    halo = shifted(after(bundle, two), "seq", 1)
    sixteen = shifted(after(far[4], one), "seq", 16)
    return [one, two, four, eight, sixteen, back], halo


def shards(tokens, norm_gain, in_weight, in_bias, out_weight, out_bias):
    width, local_rows = tokens.shape
    half_rows = local_rows // 2
    hidden = in_weight.shape[1]
    short_count = short_tracks(local_rows)
    far_count = TRACKS - 1 - short_count
    near_rows = (1 + short_count) * TRACK_CH
    one = jax.ShapeDtypeStruct((TRACK_CH, local_rows), BF16)
    near_shape = jax.ShapeDtypeStruct((near_rows, local_rows), BF16)
    half_shapes = [
        jax.ShapeDtypeStruct((near_rows, half_rows), BF16),
        jax.ShapeDtypeStruct((8, half_rows), F32),
        jax.ShapeDtypeStruct((hidden, half_rows), BF16),
    ]
    far = pl.pallas_call(
        functools.partial(split_kernel, near_rows),
        out_shape=[one] * far_count,
        in_specs=[pl.BlockSpec(memory_space=pl.ANY)],
        out_specs=[VMEM] * far_count,
        scratch_shapes=[pltpu.SemaphoreType.DMA] * far_count,
        name="split",
    )(tokens)
    bundle = pl.pallas_call(
        functools.partial(halo_kernel, local_rows, short_count),
        out_shape=one,
        grid=(1,),
        in_specs=[pl.BlockSpec((near_rows, local_rows // 2), lambda i: (0, 1))],
        out_specs=pl.BlockSpec((TRACK_CH, local_rows), lambda i: (0, 0)),
        name="halo",
    )(after(tokens, far[0]))
    near = tokens[:near_rows]
    firsts = first_moves(far)
    for block_no in range(BLOCKS):
        last = block_no == BLOCKS - 1
        gain = norm_gain[block_no][:, None]
        w_in, b_in = in_weight[block_no], in_bias[block_no][:, None]
        w_out, b_out = out_weight[block_no], out_bias[block_no][:, None]
        moved, halo = last_moves(far, firsts, bundle)
        high = call(functools.partial(near_kernel, short_count, half_rows), half_shapes, 3, "high", LIMITS[0])(
            after(near, firsts[4]), gain, w_in
        )
        low = call(functools.partial(near_kernel, short_count, 0), half_shapes, 4, "low", LIMITS[0])(
            near, gain, w_in, halo
        )
        out_shape = [jax.ShapeDtypeStruct((width, local_rows), BF16)]
        if not last:
            out_shape = [jax.ShapeDtypeStruct((hidden, local_rows), BF16)] + [one] * far_count
        outs = call(functools.partial(far_kernel, near_rows, last), out_shape, 17, "far", LIMITS[1])(
            *low, *high, *moved, gain, w_in, b_in, w_out, b_out
        )
        if last:
            return outs[0]
        active, far = outs[0], outs[1:]
        firsts = first_moves(far)
        near, bundle = call(
            functools.partial(out_kernel, short_count), [near_shape, one], 5, "out", 20
        )(low[0], high[0], after(active, firsts[4]), w_out, b_out)


def solution(mesh):
    return jax.shard_map(
        shards,
        mesh=mesh,
        in_specs=(P("batch", "seq"), P(), P(), P(), P(), P()),
        out_specs=P("batch", "seq"),
        check_vma=False,
    )
```

```python
import functools

import jax
import jax.numpy as jnp
from jax import lax
from jax.experimental import pallas as pl
from jax.experimental.pallas import tpu as pltpu
from jax.sharding import PartitionSpec as P

TRACK_CH = 16
TRACKS = 19
BLOCKS = 2
LANES = 128
NEAR_TILE = 1024
TILE = 2048
COST = 1
GELU_A = 0.7978845608028654
ALPHA = (GELU_A * 0.044715) ** (1.0 / 3.0)
GELU_C = GELU_A / ALPHA
F32, BF16 = jnp.float32, jnp.bfloat16
VMEM = pl.BlockSpec(memory_space=pltpu.VMEM)


def shifted(value, axis, steps):
    count = lax.axis_size(axis)
    pairs = [(source, (source + steps) % count) for source in range(count)]
    return lax.ppermute(value, axis, pairs)


def after(value, *others):
    return lax.optimization_barrier((value, *others))[0]


def short_tracks(local_rows):
    count = 0
    while count + 1 < TRACKS and 2**count < local_rows:
        count = count + 1
    return count


def pack_halo(track, store, local_rows, short_count):
    lane = lax.broadcasted_iota(jnp.int32, (TRACK_CH, LANES), 1)
    packed = jnp.zeros((TRACK_CH, LANES), F32)
    for slot in range(short_count):
        offset = 2**slot
        if offset < LANES:
            last = track(1 + slot, local_rows - LANES, local_rows).astype(F32)
            moved = pltpu.roll(last, (2 * offset - 1) % LANES, 1)
            inside = (lane >= offset - 1) & (lane < 2 * offset - 1)
            packed = jnp.where(inside, moved, packed)
        else:
            store(offset, 2 * offset, track(1 + slot, local_rows - offset, local_rows))
    store(0, LANES, packed.astype(BF16))


def rotated_piece(track, halo, slot, begin, end):
    offset = 2**slot
    if offset < LANES:
        if begin == 0:
            packed = halo(0, LANES).astype(F32)
            before = pltpu.roll(packed, (LANES + 1 - 2 * offset) % LANES, 1)
            window = jnp.concatenate([before, track(1 + slot, 0, end).astype(F32)], 1)
        else:
            window = track(1 + slot, begin - LANES, end).astype(F32)
        return pltpu.roll(window, offset, 1)[:, LANES:].astype(BF16)
    parts = []
    if begin < offset:
        parts.append(halo(offset + begin, offset + min(end, offset)))
    if end > offset:
        parts.append(track(1 + slot, max(begin, offset) - offset, end - offset))
    return parts[0] if len(parts) == 1 else jnp.concatenate(parts, 1)


def split_kernel(first_row, tokens, *refs):
    count = len(refs) // 2
    copies = []
    for at in range(count):
        top = first_row + at * TRACK_CH
        copies.append(
            pltpu.make_async_copy(tokens.at[top : top + TRACK_CH, :], refs[at], refs[count + at])
        )
    for copy in copies:
        copy.start()
    for copy in copies:
        copy.wait()


def pair_kernel(short_count, tokens, out, tail, sem, own_sem):
    near_rows, half_rows = tail.shape
    local_rows = out.shape[1]
    base = local_rows - half_rows
    copy = pltpu.make_async_copy(tokens.at[:near_rows, base:], tail, sem)
    own = pltpu.make_async_copy(
        tokens.at[near_rows : near_rows + TRACK_CH, :], out.at[TRACK_CH:, :], own_sem
    )
    copy.start()
    own.start()
    copy.wait()

    def track(t, begin, end):
        return tail[t * TRACK_CH : (t + 1) * TRACK_CH, begin - base : end - base]

    def store(begin, end, value):
        out[:TRACK_CH, begin:end] = value

    pack_halo(track, store, local_rows, short_count)
    own.wait()


def weight_kernel(transposed, bias, *outs):
    depth, hidden = transposed.shape[1:]
    row = lax.broadcasted_iota(jnp.int32, (TRACK_CH, hidden), 0)
    for block_no, out in enumerate(outs):
        left = bias[block_no : block_no + 1, :] * ALPHA
        rows = jnp.zeros((TRACK_CH, hidden), F32)
        for at in range(3):
            term = left.astype(BF16).astype(F32)
            rows = jnp.where(row == at, jnp.broadcast_to(term, rows.shape), rows)
            left = left - term
        joined = jnp.concatenate([transposed[block_no], rows.astype(BF16)], 0)
        out[...] = jnp.transpose(joined)


def near_kernel(short_count, near, halo_in, rotated, squares):
    local_rows = halo_in.shape[1]

    def track(t, begin, end):
        return near[t * TRACK_CH : (t + 1) * TRACK_CH, begin:end]

    def halo(begin, end):
        return halo_in[:TRACK_CH, begin:end]

    for begin in range(0, local_rows, NEAR_TILE):
        end = begin + NEAR_TILE
        total = jnp.zeros((8, NEAR_TILE), F32)
        for t in range(1 + short_count):
            piece = track(0, begin, end) if t == 0 else rotated_piece(track, halo, t - 1, begin, end)
            rotated[t * TRACK_CH : (t + 1) * TRACK_CH, begin:end] = piece
            piece = piece.astype(F32)
            total = total + (piece[:8] * piece[:8] + piece[8:] * piece[8:])
        squares[:, begin:end] = total


def main_kernel(short_count, block_no, last, near, squares, pair, *refs):
    far, (gain, w_in, w_out, b_out), outs = refs[:5], refs[5:9], refs[9:]
    near_rows, local_rows = near.shape
    width = near_rows + (1 + len(far)) * TRACK_CH
    ones = jnp.ones((TRACK_CH, TILE), BF16)
    for begin in range(0, local_rows, TILE):
        end = begin + TILE
        parts = [pair[TRACK_CH:, begin:end].astype(F32)]
        parts += [ref[:, begin:end].astype(F32) for ref in far]
        total = squares[:, begin:end]
        for part in parts:
            total = total + (part[:8] * part[:8] + part[8:] * part[8:])
        scale = ALPHA * lax.rsqrt(jnp.sum(total, axis=0, keepdims=True) * (1.0 / width) + 1e-06)
        rotated = jnp.concatenate([near[:, begin:end].astype(F32)] + parts, 0)
        normed = (rotated * gain[...] * scale).astype(BF16)
        pre = jnp.dot(w_in[...], jnp.concatenate([normed, ones], 0), preferred_element_type=F32)
        inner = pre * (GELU_C + pre * pre)
        active = (pre * (1.0 + jnp.tanh(inner))).astype(BF16)
        out = jnp.dot(w_out[block_no], active, preferred_element_type=F32)
        mixed = (rotated + out * (0.5 / ALPHA) + b_out[...]).astype(BF16)
        if last:
            outs[0][:, begin:end] = mixed
        else:
            outs[0][:, begin:end] = mixed[:near_rows]
            outs[1][TRACK_CH:, begin:end] = mixed[near_rows : near_rows + TRACK_CH]
            for at in range(len(far)):
                top = near_rows + (1 + at) * TRACK_CH
                outs[2 + at][:, begin:end] = mixed[top : top + TRACK_CH]
    if not last:

        def track(t, begin, end):
            return outs[0][t * TRACK_CH : (t + 1) * TRACK_CH, begin:end]

        def store(begin, end, value):
            outs[1][:TRACK_CH, begin:end] = value

        pack_halo(track, store, local_rows, short_count)


def call(kernel, out_shape, in_specs, name, limit):
    return pl.pallas_call(
        kernel,
        out_shape=out_shape,
        in_specs=in_specs,
        out_specs=[VMEM] * len(out_shape),
        compiler_params=pltpu.CompilerParams(vmem_limit_bytes=limit << 20),
        cost_estimate=pl.CostEstimate(flops=COST, transcendentals=0, bytes_accessed=COST),
        name=name,
    )


def permuted(value, moves):
    return lax.ppermute(value, "seq", moves)


def routes():
    first, second = [], []
    for y in range(4):
        for z in range(8):
            for x in range(2):
                source = (y * 8 + z) * 2 + x
                middle = (((y + z // 4) % 4) * 8 + (z - 2) % 8) * 2 + x
                first.append((source, middle))
                second.append((middle, (source + 8) % 64))
    return first, second


def exchange(pair, far):
    two, four, eight, sixteen, thirty_two = far
    to_middle, from_middle = routes()
    eight = permuted(eight, to_middle)
    pair = shifted(pair, "seq", 1)
    back = shifted(thirty_two, "seq", -16)
    four = shifted(four, "seq", 4)
    two = shifted(two, "seq", 2)
    eight = permuted(eight, from_middle)
    back = shifted(back, "seq", -16)
    sixteen = shifted(after(sixteen, two), "seq", 16)
    return pair, [two, four, eight, sixteen, back]


def shards(tokens, norm_gain, in_weight, in_bias, out_weight, out_bias):
    width, local_rows = tokens.shape
    hidden = in_weight.shape[1]
    short_count = short_tracks(local_rows)
    far_count = TRACKS - 2 - short_count
    near_rows = (1 + short_count) * TRACK_CH
    one = jax.ShapeDtypeStruct((TRACK_CH, local_rows), BF16)
    two = jax.ShapeDtypeStruct((2 * TRACK_CH, local_rows), BF16)
    near_shape = jax.ShapeDtypeStruct((near_rows, local_rows), BF16)
    squares_shape = jax.ShapeDtypeStruct((8, local_rows), F32)
    whole = pl.BlockSpec(memory_space=pl.ANY)
    far = pl.pallas_call(
        functools.partial(split_kernel, near_rows + TRACK_CH),
        out_shape=[one] * far_count,
        in_specs=[whole],
        out_specs=[whole] * far_count,
        scratch_shapes=[pltpu.SemaphoreType.DMA] * far_count,
        name="split",
    )(tokens)
    pair = pl.pallas_call(
        functools.partial(pair_kernel, short_count),
        out_shape=two,
        in_specs=[whole],
        out_specs=VMEM,
        scratch_shapes=[
            pltpu.VMEM((near_rows, local_rows // 2), BF16),
            pltpu.SemaphoreType.DMA,
            pltpu.SemaphoreType.DMA,
        ],
        name="pair",
    )(tokens)
    w_ins = call(
        weight_kernel, [jax.ShapeDtypeStruct((hidden, width + TRACK_CH), BF16)] * BLOCKS, [VMEM] * 2, "weights", 8
    )(jnp.swapaxes(in_weight, 1, 2), in_bias)
    near = tokens
    for block_no in range(BLOCKS):
        last = block_no == BLOCKS - 1
        pair, moved = exchange(pair, far)
        rotated, squares = call(
            functools.partial(near_kernel, short_count), [near_shape, squares_shape], [VMEM] * 2, "near", 8
        )(near, pair)
        out_shape = [jax.ShapeDtypeStruct((width, local_rows), BF16)]
        if not last:
            out_shape = [near_shape, two] + [one] * far_count
        outs = call(
            functools.partial(main_kernel, short_count, block_no, last),
            out_shape,
            [VMEM] * (7 + far_count),
            "main",
            24,
        )(rotated, squares, pair, *moved, norm_gain[block_no][:, None], w_ins[block_no], out_weight, out_bias[block_no][:, None])
        if last:
            return outs[0]
        near, pair, far = outs[0], outs[1], outs[2:]


def solution(mesh):
    return jax.shard_map(
        shards,
        mesh=mesh,
        in_specs=(P("batch", "seq"), P(), P(), P(), P(), P()),
        out_specs=P("batch", "seq"),
        check_vma=False,
    )
```

```python
import functools

import jax
import jax.numpy as jnp
from jax import lax
from jax.experimental import pallas as pl
from jax.experimental.pallas import tpu as pltpu
from jax.sharding import PartitionSpec as P

TRACK_CH = 16
TRACKS = 19
BLOCKS = 2
LANES = 128
NEAR_TILE = 1024
TILE = 2048
COST = 1
GELU_A = 0.7978845608028654
ALPHA = (GELU_A * 0.044715) ** (1.0 / 3.0)
GELU_C = GELU_A / ALPHA
F32, BF16 = jnp.float32, jnp.bfloat16
VMEM = pl.BlockSpec(memory_space=pltpu.VMEM)


def shifted(value, axis, steps):
    count = lax.axis_size(axis)
    pairs = [(source, (source + steps) % count) for source in range(count)]
    return lax.ppermute(value, axis, pairs)


def after(value, *others):
    return lax.optimization_barrier((value, *others))[0]


def short_tracks(local_rows):
    count = 0
    while count + 1 < TRACKS and 2**count < local_rows:
        count = count + 1
    return count


def pack_halo(track, store, local_rows, short_count):
    lane = lax.broadcasted_iota(jnp.int32, (TRACK_CH, LANES), 1)
    packed = jnp.zeros((TRACK_CH, LANES), F32)
    for slot in range(short_count):
        offset = 2**slot
        if offset < LANES:
            last = track(1 + slot, local_rows - LANES, local_rows).astype(F32)
            moved = pltpu.roll(last, (2 * offset - 1) % LANES, 1)
            inside = (lane >= offset - 1) & (lane < 2 * offset - 1)
            packed = jnp.where(inside, moved, packed)
        else:
            store(offset, 2 * offset, track(1 + slot, local_rows - offset, local_rows))
    store(0, LANES, packed.astype(BF16))


def rotated_piece(track, halo, slot, begin, end):
    offset = 2**slot
    if offset < LANES:
        if begin == 0:
            packed = halo(0, LANES).astype(F32)
            before = pltpu.roll(packed, (LANES + 1 - 2 * offset) % LANES, 1)
            window = jnp.concatenate([before, track(1 + slot, 0, end).astype(F32)], 1)
        else:
            window = track(1 + slot, begin - LANES, end).astype(F32)
        return pltpu.roll(window, offset, 1)[:, LANES:].astype(BF16)
    parts = []
    if begin < offset:
        parts.append(halo(offset + begin, offset + min(end, offset)))
    if end > offset:
        parts.append(track(1 + slot, max(begin, offset) - offset, end - offset))
    return parts[0] if len(parts) == 1 else jnp.concatenate(parts, 1)


def first_kernel(short_count, tokens, *refs):
    pair, far = refs[0], refs[1:6]
    tail, sems = refs[6], refs[7:]
    near_rows, half_rows = tail.shape
    local_rows = pair.shape[1]
    base = local_rows - half_rows
    copies = [pltpu.make_async_copy(tokens.at[:near_rows, base:], tail, sems[0])]
    for at, target in enumerate([pair.at[TRACK_CH:, :], *far]):
        top = near_rows + at * TRACK_CH
        copies.append(
            pltpu.make_async_copy(tokens.at[top : top + TRACK_CH, :], target, sems[1 + at])
        )
    for copy in copies:
        copy.start()
    copies[0].wait()

    def track(t, begin, end):
        return tail[t * TRACK_CH : (t + 1) * TRACK_CH, begin - base : end - base]

    def store(begin, end, value):
        pair[:TRACK_CH, begin:end] = value

    pack_halo(track, store, local_rows, short_count)
    for copy in copies[1:]:
        copy.wait()


def weight_kernel(transposed, bias, gain, last_bias, *refs):
    outs, made, sems = refs[:3], refs[3:6], refs[6:]
    depth, hidden = transposed.shape[1:]
    row = lax.broadcasted_iota(jnp.int32, (TRACK_CH, hidden), 0)
    copies = []
    for block_no in range(BLOCKS):
        left = bias[block_no : block_no + 1, :] * ALPHA
        rows = jnp.zeros((TRACK_CH, hidden), F32)
        for at in range(3):
            term = left.astype(BF16).astype(F32)
            rows = jnp.where(row == at, jnp.broadcast_to(term, rows.shape), rows)
            left = left - term
        joined = jnp.concatenate([transposed[block_no], rows.astype(BF16)], 0)
        made[block_no][...] = jnp.transpose(joined)
        copies.append(pltpu.make_async_copy(made[block_no], outs[block_no], sems[block_no]))
        copies[-1].start()
    columns = [gain[...], last_bias[...], jnp.zeros((8 - 2 * BLOCKS, depth), F32)]
    made[2][...] = jnp.transpose(jnp.concatenate(columns, 0))
    copies.append(pltpu.make_async_copy(made[2], outs[2], sems[2]))
    copies[-1].start()
    for copy in copies:
        copy.wait()


def near_kernel(short_count, near, halo_in, rotated, squares):
    local_rows = halo_in.shape[1]

    def track(t, begin, end):
        return near[t * TRACK_CH : (t + 1) * TRACK_CH, begin:end]

    def halo(begin, end):
        return halo_in[:TRACK_CH, begin:end]

    for begin in range(0, local_rows, NEAR_TILE):
        end = begin + NEAR_TILE
        total = jnp.zeros((8, NEAR_TILE), F32)
        for t in range(1 + short_count):
            piece = track(0, begin, end) if t == 0 else rotated_piece(track, halo, t - 1, begin, end)
            rotated[t * TRACK_CH : (t + 1) * TRACK_CH, begin:end] = piece
            piece = piece.astype(F32)
            total = total + (piece[:8] * piece[:8] + piece[8:] * piece[8:])
        squares[:, begin:end] = total


def main_kernel(short_count, block_no, last, near, squares, pair, *refs):
    far, (columns, w_in, w_out), outs = refs[:5], refs[5:8], refs[8:]
    near_rows, local_rows = near.shape
    width = near_rows + (1 + len(far)) * TRACK_CH
    ones = jnp.ones((TRACK_CH, TILE), BF16)
    gain = columns[:, block_no : block_no + 1]
    b_out = columns[:, BLOCKS + block_no : BLOCKS + block_no + 1]
    for begin in range(0, local_rows, TILE):
        end = begin + TILE
        parts = [pair[TRACK_CH:, begin:end].astype(F32)]
        parts += [ref[:, begin:end].astype(F32) for ref in far]
        total = squares[:, begin:end]
        for part in parts:
            total = total + (part[:8] * part[:8] + part[8:] * part[8:])
        scale = ALPHA * lax.rsqrt(jnp.sum(total, axis=0, keepdims=True) * (1.0 / width) + 1e-06)
        rotated = jnp.concatenate([near[:, begin:end].astype(F32)] + parts, 0)
        normed = (rotated * gain * scale).astype(BF16)
        pre = jnp.dot(w_in[...], jnp.concatenate([normed, ones], 0), preferred_element_type=F32)
        inner = pre * (GELU_C + pre * pre)
        active = (pre * (1.0 + jnp.tanh(inner))).astype(BF16)
        out = jnp.dot(w_out[block_no], active, preferred_element_type=F32)
        mixed = (rotated + out * (0.5 / ALPHA) + b_out).astype(BF16)
        if last:
            outs[0][:, begin:end] = mixed
        else:
            outs[0][:, begin:end] = mixed[:near_rows]
            outs[1][TRACK_CH:, begin:end] = mixed[near_rows : near_rows + TRACK_CH]
            for at in range(len(far)):
                top = near_rows + (1 + at) * TRACK_CH
                outs[2 + at][:, begin:end] = mixed[top : top + TRACK_CH]
    if not last:

        def track(t, begin, end):
            return outs[0][t * TRACK_CH : (t + 1) * TRACK_CH, begin:end]

        def store(begin, end, value):
            outs[1][:TRACK_CH, begin:end] = value

        pack_halo(track, store, local_rows, short_count)


def call(kernel, out_shape, in_specs, name, limit):
    return pl.pallas_call(
        kernel,
        out_shape=out_shape,
        in_specs=in_specs,
        out_specs=[VMEM] * len(out_shape),
        compiler_params=pltpu.CompilerParams(vmem_limit_bytes=limit << 20),
        cost_estimate=pl.CostEstimate(flops=COST, transcendentals=0, bytes_accessed=COST),
        name=name,
    )


def permuted(value, moves):
    return lax.ppermute(value, "seq", moves)


def routes():
    first, second = [], []
    for y in range(4):
        for z in range(8):
            for x in range(2):
                source = (y * 8 + z) * 2 + x
                middle = (((y + z // 4) % 4) * 8 + (z - 2) % 8) * 2 + x
                first.append((source, middle))
                second.append((middle, (source + 8) % 64))
    return first, second


def exchange(pair, far):
    two, four, eight, sixteen, thirty_two = far
    to_middle, from_middle = routes()
    eight = permuted(eight, to_middle)
    pair = shifted(pair, "seq", 1)
    back = shifted(thirty_two, "seq", -16)
    four = shifted(four, "seq", 4)
    two = shifted(two, "seq", 2)
    eight = permuted(eight, from_middle)
    back = shifted(back, "seq", -16)
    sixteen = shifted(after(sixteen, two), "seq", 16)
    return pair, [two, four, eight, sixteen, back]


def shards(tokens, norm_gain, in_weight, in_bias, out_weight, out_bias):
    width, local_rows = tokens.shape
    hidden = in_weight.shape[1]
    short_count = short_tracks(local_rows)
    far_count = TRACKS - 2 - short_count
    near_rows = (1 + short_count) * TRACK_CH
    one = jax.ShapeDtypeStruct((TRACK_CH, local_rows), BF16)
    two = jax.ShapeDtypeStruct((2 * TRACK_CH, local_rows), BF16)
    near_shape = jax.ShapeDtypeStruct((near_rows, local_rows), BF16)
    squares_shape = jax.ShapeDtypeStruct((8, local_rows), F32)
    whole = pl.BlockSpec(memory_space=pl.ANY)
    pair, *far = pl.pallas_call(
        functools.partial(first_kernel, short_count),
        out_shape=[two] + [one] * far_count,
        in_specs=[pl.BlockSpec(memory_space=pl.ANY)],
        out_specs=[VMEM] * (1 + far_count),
        scratch_shapes=[pltpu.VMEM((near_rows, local_rows // 2), BF16)]
        + [pltpu.SemaphoreType.DMA] * (2 + far_count),
        name="first",
    )(tokens)
    made = [((hidden, width + TRACK_CH), BF16)] * BLOCKS + [((width, 8), F32)]
    *w_ins, columns = pl.pallas_call(
        weight_kernel,
        out_shape=[jax.ShapeDtypeStruct(*entry) for entry in made],
        in_specs=[VMEM] * 4,
        out_specs=[pl.BlockSpec(memory_space=pltpu.HBM)] * 3,
        scratch_shapes=[pltpu.VMEM(*entry) for entry in made] + [pltpu.SemaphoreType.DMA] * 3,
        name="weights",
    )(jnp.swapaxes(in_weight, 1, 2), in_bias, norm_gain, out_bias)
    near = tokens
    for block_no in range(BLOCKS):
        last = block_no == BLOCKS - 1
        pair, moved = exchange(pair, far)
        rotated, squares = call(
            functools.partial(near_kernel, short_count), [near_shape, squares_shape], [VMEM] * 2, "near", 8
        )(near, pair)
        out_shape = [jax.ShapeDtypeStruct((width, local_rows), BF16)]
        if not last:
            out_shape = [near_shape, two] + [one] * far_count
        outs = call(
            functools.partial(main_kernel, short_count, block_no, last),
            out_shape,
            [VMEM] * (6 + far_count),
            "main",
            24,
        )(rotated, squares, pair, *moved, columns, w_ins[block_no], out_weight)
        if last:
            return outs[0]
        near, pair, far = outs[0], outs[1], outs[2:]


def solution(mesh):
    return jax.shard_map(
        shards,
        mesh=mesh,
        in_specs=(P("batch", "seq"), P(), P(), P(), P(), P()),
        out_specs=P("batch", "seq"),
        check_vma=False,
    )
```

```python
import functools

import jax
import jax.numpy as jnp
from jax import lax
from jax.experimental import pallas as pl
from jax.experimental.pallas import tpu as pltpu
from jax.sharding import PartitionSpec as P

TRACK_CH = 16
TRACKS = 19
BLOCKS = 2
LANES = 128
NEAR_TILE = 1024
TILE = 2048
COST = 1
GELU_A = 0.7978845608028654
ALPHA = (GELU_A * 0.044715) ** (1.0 / 3.0)
GELU_C = GELU_A / ALPHA
F32, BF16 = jnp.float32, jnp.bfloat16
VMEM = pl.BlockSpec(memory_space=pltpu.VMEM)


def shifted(value, axis, steps):
    count = lax.axis_size(axis)
    pairs = [(source, (source + steps) % count) for source in range(count)]
    return lax.ppermute(value, axis, pairs)


def after(value, *others):
    return lax.optimization_barrier((value, *others))[0]


def short_tracks(local_rows):
    count = 0
    while count + 1 < TRACKS and 2**count < local_rows:
        count = count + 1
    return count


def pack_halo(track, store, local_rows, short_count):
    lane = lax.broadcasted_iota(jnp.int32, (TRACK_CH, LANES), 1)
    packed = jnp.zeros((TRACK_CH, LANES), F32)
    for slot in range(short_count):
        offset = 2**slot
        if offset < LANES:
            last = track(1 + slot, local_rows - LANES, local_rows).astype(F32)
            moved = pltpu.roll(last, (2 * offset - 1) % LANES, 1)
            inside = (lane >= offset - 1) & (lane < 2 * offset - 1)
            packed = jnp.where(inside, moved, packed)
        else:
            store(offset, 2 * offset, track(1 + slot, local_rows - offset, local_rows))
    store(0, LANES, packed.astype(BF16))


def rotated_piece(track, halo, slot, begin, end):
    offset = 2**slot
    if offset < LANES:
        if begin == 0:
            packed = halo(0, LANES).astype(F32)
            before = pltpu.roll(packed, (LANES + 1 - 2 * offset) % LANES, 1)
            window = jnp.concatenate([before, track(1 + slot, 0, end).astype(F32)], 1)
        else:
            window = track(1 + slot, begin - LANES, end).astype(F32)
        return pltpu.roll(window, offset, 1)[:, LANES:].astype(BF16)
    parts = []
    if begin < offset:
        parts.append(halo(offset + begin, offset + min(end, offset)))
    if end > offset:
        parts.append(track(1 + slot, max(begin, offset) - offset, end - offset))
    return parts[0] if len(parts) == 1 else jnp.concatenate(parts, 1)


def first_kernel(short_count, tokens, *refs):
    pair, duo, far = refs[0], refs[1], refs[2:5]
    tail, sems = refs[5], refs[6:]
    near_rows, half_rows = tail.shape
    local_rows = pair.shape[1]
    base = local_rows - half_rows
    copies = [pltpu.make_async_copy(tokens.at[:near_rows, base:], tail, sems[0])]
    for at, target in enumerate([pair.at[TRACK_CH:, :], duo.at[:TRACK_CH, :], duo.at[TRACK_CH:, :], *far]):
        top = near_rows + at * TRACK_CH
        copies.append(
            pltpu.make_async_copy(tokens.at[top : top + TRACK_CH, :], target, sems[1 + at])
        )
    for copy in copies:
        copy.start()
    copies[0].wait()

    def track(t, begin, end):
        return tail[t * TRACK_CH : (t + 1) * TRACK_CH, begin - base : end - base]

    def store(begin, end, value):
        pair[:TRACK_CH, begin:end] = value

    pack_halo(track, store, local_rows, short_count)
    for copy in copies[1:]:
        copy.wait()


def weight_kernel(transposed, bias, gain, last_bias, *refs):
    outs, made, sems = refs[:3], refs[3:6], refs[6:]
    depth, hidden = transposed.shape[1:]
    row = lax.broadcasted_iota(jnp.int32, (TRACK_CH, hidden), 0)
    copies = []
    for block_no in range(BLOCKS):
        left = bias[block_no : block_no + 1, :] * ALPHA
        rows = jnp.zeros((TRACK_CH, hidden), F32)
        for at in range(3):
            term = left.astype(BF16).astype(F32)
            rows = jnp.where(row == at, jnp.broadcast_to(term, rows.shape), rows)
            left = left - term
        joined = jnp.concatenate([transposed[block_no], rows.astype(BF16)], 0)
        made[block_no][...] = jnp.transpose(joined)
        copies.append(pltpu.make_async_copy(made[block_no], outs[block_no], sems[block_no]))
        copies[-1].start()
    columns = [gain[...], last_bias[...], jnp.zeros((8 - 2 * BLOCKS, depth), F32)]
    made[2][...] = jnp.transpose(jnp.concatenate(columns, 0))
    copies.append(pltpu.make_async_copy(made[2], outs[2], sems[2]))
    copies[-1].start()
    for copy in copies:
        copy.wait()


def near_kernel(short_count, near, halo_in, rotated, squares):
    local_rows = halo_in.shape[1]

    def track(t, begin, end):
        return near[t * TRACK_CH : (t + 1) * TRACK_CH, begin:end]

    def halo(begin, end):
        return halo_in[:TRACK_CH, begin:end]

    for begin in range(0, local_rows, NEAR_TILE):
        end = begin + NEAR_TILE
        total = jnp.zeros((8, NEAR_TILE), F32)
        for t in range(1 + short_count):
            piece = track(0, begin, end) if t == 0 else rotated_piece(track, halo, t - 1, begin, end)
            rotated[t * TRACK_CH : (t + 1) * TRACK_CH, begin:end] = piece
            piece = piece.astype(F32)
            total = total + (piece[:8] * piece[:8] + piece[8:] * piece[8:])
        squares[:, begin:end] = total


def main_kernel(short_count, block_no, last, near, squares, pair, *refs):
    far, (columns, w_in, w_out), outs = refs[:5], refs[5:8], refs[8:]
    near_rows, local_rows = near.shape
    width = near_rows + (1 + len(far)) * TRACK_CH
    ones = jnp.ones((TRACK_CH, TILE), BF16)
    gain = columns[:, block_no : block_no + 1]
    b_out = columns[:, BLOCKS + block_no : BLOCKS + block_no + 1]
    for begin in range(0, local_rows, TILE):
        end = begin + TILE
        parts = [pair[TRACK_CH:, begin:end].astype(F32)]
        parts += [ref[:TRACK_CH, begin:end].astype(F32) for ref in far]
        total = squares[:, begin:end]
        for part in parts:
            total = total + (part[:8] * part[:8] + part[8:] * part[8:])
        scale = ALPHA * lax.rsqrt(jnp.sum(total, axis=0, keepdims=True) * (1.0 / width) + 1e-06)
        rotated = jnp.concatenate([near[:, begin:end].astype(F32)] + parts, 0)
        normed = (rotated * gain * scale).astype(BF16)
        pre = jnp.dot(w_in[...], jnp.concatenate([normed, ones], 0), preferred_element_type=F32)
        inner = pre * (GELU_C + pre * pre)
        active = (pre * (1.0 + jnp.tanh(inner))).astype(BF16)
        out = jnp.dot(w_out[block_no], active, preferred_element_type=F32)
        mixed = (rotated + out * (0.5 / ALPHA) + b_out).astype(BF16)
        if last:
            outs[0][:, begin:end] = mixed
        else:
            outs[0][:, begin:end] = mixed[:near_rows]
            outs[1][TRACK_CH:, begin:end] = mixed[near_rows : near_rows + TRACK_CH]
            outs[2][:, begin:end] = mixed[near_rows + TRACK_CH : near_rows + 3 * TRACK_CH]
            for at in range(3):
                top = near_rows + (3 + at) * TRACK_CH
                outs[3 + at][:, begin:end] = mixed[top : top + TRACK_CH]
    if not last:

        def track(t, begin, end):
            return outs[0][t * TRACK_CH : (t + 1) * TRACK_CH, begin:end]

        def store(begin, end, value):
            outs[1][:TRACK_CH, begin:end] = value

        pack_halo(track, store, local_rows, short_count)


def call(kernel, out_shape, in_specs, name, limit):
    return pl.pallas_call(
        kernel,
        out_shape=out_shape,
        in_specs=in_specs,
        out_specs=[VMEM] * len(out_shape),
        compiler_params=pltpu.CompilerParams(vmem_limit_bytes=limit << 20),
        cost_estimate=pl.CostEstimate(flops=COST, transcendentals=0, bytes_accessed=COST),
        name=name,
    )


def permuted(value, moves):
    return lax.ppermute(value, "seq", moves)


def routes():
    first, second = [], []
    for y in range(4):
        for z in range(8):
            for x in range(2):
                source = (y * 8 + z) * 2 + x
                middle = (((y + z // 4) % 4) * 8 + (z - 2) % 8) * 2 + x
                first.append((source, middle))
                second.append((middle, (source + 8) % 64))
    return first, second


def exchange(pair, duo, far):
    eight, sixteen, thirty_two = far
    to_middle, from_middle = routes()
    eight = permuted(eight, to_middle)
    duo = shifted(duo, "seq", 2)
    pair = shifted(pair, "seq", 1)
    back = shifted(thirty_two, "seq", -16)
    sixteen = shifted(sixteen, "seq", 16)
    four = shifted(after(duo[TRACK_CH:], eight), "seq", 2)
    back = shifted(after(back, duo), "seq", -16)
    eight = permuted(eight, from_middle)
    return pair, [duo, four, eight, sixteen, back]


def shards(tokens, norm_gain, in_weight, in_bias, out_weight, out_bias):
    width, local_rows = tokens.shape
    hidden = in_weight.shape[1]
    short_count = short_tracks(local_rows)
    far_count = TRACKS - 2 - short_count
    near_rows = (1 + short_count) * TRACK_CH
    one = jax.ShapeDtypeStruct((TRACK_CH, local_rows), BF16)
    two = jax.ShapeDtypeStruct((2 * TRACK_CH, local_rows), BF16)
    near_shape = jax.ShapeDtypeStruct((near_rows, local_rows), BF16)
    squares_shape = jax.ShapeDtypeStruct((8, local_rows), F32)
    whole = pl.BlockSpec(memory_space=pl.ANY)
    pair, duo, *far = pl.pallas_call(
        functools.partial(first_kernel, short_count),
        out_shape=[two] * 2 + [one] * (far_count - 2),
        in_specs=[pl.BlockSpec(memory_space=pl.ANY)],
        out_specs=[VMEM] * far_count,
        scratch_shapes=[pltpu.VMEM((near_rows, local_rows // 2), BF16)]
        + [pltpu.SemaphoreType.DMA] * (2 + far_count),
        name="first",
    )(tokens)
    made = [((hidden, width + TRACK_CH), BF16)] * BLOCKS + [((width, 8), F32)]
    *w_ins, columns = pl.pallas_call(
        weight_kernel,
        out_shape=[jax.ShapeDtypeStruct(*entry) for entry in made],
        in_specs=[VMEM] * 4,
        out_specs=[pl.BlockSpec(memory_space=pltpu.HBM)] * 3,
        scratch_shapes=[pltpu.VMEM(*entry) for entry in made] + [pltpu.SemaphoreType.DMA] * 3,
        name="weights",
    )(jnp.swapaxes(in_weight, 1, 2), in_bias, norm_gain, out_bias)
    near = tokens
    for block_no in range(BLOCKS):
        last = block_no == BLOCKS - 1
        pair, moved = exchange(pair, duo, far)
        rotated, squares = call(
            functools.partial(near_kernel, short_count), [near_shape, squares_shape], [VMEM] * 2, "near", 8
        )(near, pair)
        out_shape = [jax.ShapeDtypeStruct((width, local_rows), BF16)]
        if not last:
            out_shape = [near_shape, two, two] + [one] * (far_count - 2)
        outs = call(
            functools.partial(main_kernel, short_count, block_no, last),
            out_shape,
            [VMEM] * (6 + far_count),
            "main",
            24,
        )(rotated, squares, pair, *moved, columns, w_ins[block_no], out_weight)
        if last:
            return outs[0]
        near, pair, duo, far = outs[0], outs[1], outs[2], outs[3:]


def solution(mesh):
    return jax.shard_map(
        shards,
        mesh=mesh,
        in_specs=(P("batch", "seq"), P(), P(), P(), P(), P()),
        out_specs=P("batch", "seq"),
        check_vma=False,
    )
```

```python
import functools

import jax
import jax.numpy as jnp
from jax import lax
from jax.experimental import pallas as pl
from jax.experimental.pallas import tpu as pltpu
from jax.sharding import PartitionSpec as P

TRACK_CH = 16
TRACKS = 19
BLOCKS = 2
LANES = 128
NEAR_TILE = 1024
TILE = 2048
COST = 1
GELU_A = 0.7978845608028654
ALPHA = (GELU_A * 0.044715) ** (1.0 / 3.0)
GELU_C = GELU_A / ALPHA
F32, BF16 = jnp.float32, jnp.bfloat16
VMEM = pl.BlockSpec(memory_space=pltpu.VMEM)


def shifted(value, axis, steps):
    count = lax.axis_size(axis)
    pairs = [(source, (source + steps) % count) for source in range(count)]
    return lax.ppermute(value, axis, pairs)


def after(value, *others):
    return lax.optimization_barrier((value, *others))[0]


def short_tracks(local_rows):
    count = 0
    while count + 1 < TRACKS and 2**count < local_rows:
        count = count + 1
    return count


def pack_halo(track, store, local_rows, short_count):
    lane = lax.broadcasted_iota(jnp.int32, (TRACK_CH, LANES), 1)
    packed = jnp.zeros((TRACK_CH, LANES), F32)
    for slot in range(short_count):
        offset = 2**slot
        if offset < LANES:
            last = track(1 + slot, local_rows - LANES, local_rows).astype(F32)
            moved = pltpu.roll(last, (2 * offset - 1) % LANES, 1)
            inside = (lane >= offset - 1) & (lane < 2 * offset - 1)
            packed = jnp.where(inside, moved, packed)
        else:
            store(offset, 2 * offset, track(1 + slot, local_rows - offset, local_rows))
    store(0, LANES, packed.astype(BF16))


def rotated_piece(track, halo, slot, begin, end):
    offset = 2**slot
    if offset < LANES:
        if begin == 0:
            packed = halo(0, LANES).astype(F32)
            before = pltpu.roll(packed, (LANES + 1 - 2 * offset) % LANES, 1)
            window = jnp.concatenate([before, track(1 + slot, 0, end).astype(F32)], 1)
        else:
            window = track(1 + slot, begin - LANES, end).astype(F32)
        return pltpu.roll(window, offset, 1)[:, LANES:].astype(BF16)
    parts = []
    if begin < offset:
        parts.append(halo(offset + begin, offset + min(end, offset)))
    if end > offset:
        parts.append(track(1 + slot, max(begin, offset) - offset, end - offset))
    return parts[0] if len(parts) == 1 else jnp.concatenate(parts, 1)


def first_kernel(short_count, tokens, *refs):
    pair, duo, far = refs[0], refs[1], refs[2:5]
    tail, sems = refs[5], refs[6:]
    near_rows, half_rows = tail.shape
    local_rows = pair.shape[1]
    base = local_rows - half_rows
    copies = [pltpu.make_async_copy(tokens.at[:near_rows, base:], tail, sems[0])]
    for at, target in enumerate([pair.at[TRACK_CH:, :], duo.at[:TRACK_CH, :], duo.at[TRACK_CH:, :], *far]):
        top = near_rows + at * TRACK_CH
        copies.append(
            pltpu.make_async_copy(tokens.at[top : top + TRACK_CH, :], target, sems[1 + at])
        )
    for copy in copies:
        copy.start()
    copies[0].wait()

    def track(t, begin, end):
        return tail[t * TRACK_CH : (t + 1) * TRACK_CH, begin - base : end - base]

    def store(begin, end, value):
        pair[:TRACK_CH, begin:end] = value

    pack_halo(track, store, local_rows, short_count)
    for copy in copies[1:]:
        copy.wait()


def weight_kernel(transposed, bias, gain, last_bias, *refs):
    outs, made, sems = refs[:4], refs[4:8], refs[8:]
    depth, hidden = transposed.shape[1:]
    copies = []
    for block_no in range(BLOCKS):
        made[block_no][...] = jnp.transpose(transposed[block_no])
        copies.append(pltpu.make_async_copy(made[block_no], outs[block_no], sems[block_no]))
        copies[-1].start()
    columns = [gain[...], last_bias[...], jnp.zeros((8 - 2 * BLOCKS, depth), F32)]
    made[2][...] = jnp.transpose(jnp.concatenate(columns, 0))
    made[3][...] = jnp.transpose(jnp.concatenate([bias[...], jnp.zeros((8 - BLOCKS, hidden), F32)], 0))
    for at in (2, 3):
        copies.append(pltpu.make_async_copy(made[at], outs[at], sems[at]))
        copies[-1].start()
    for copy in copies:
        copy.wait()


def near_kernel(short_count, block_no, first, near, columns, w_in, *refs):
    halo_in = refs[0]
    rotated, squares, partial = refs[-3:]
    near_rows, width = rotated.shape
    gain = columns[:near_rows, block_no : block_no + 1]

    def track(t, begin, end):
        return near[t * TRACK_CH : (t + 1) * TRACK_CH, begin:end]

    def halo(begin, end):
        return halo_in[:TRACK_CH, begin:end]

    for at in range(0, width, NEAR_TILE):
        begin, end = first + at, first + at + NEAR_TILE
        total = jnp.zeros((8, NEAR_TILE), F32)
        scaled = []
        for t in range(1 + short_count):
            rows = slice(t * TRACK_CH, (t + 1) * TRACK_CH)
            piece = track(0, begin, end) if t == 0 else rotated_piece(track, halo, t - 1, begin, end)
            rotated[rows, at : at + NEAR_TILE] = piece
            piece = piece.astype(F32)
            total = total + (piece[:8] * piece[:8] + piece[8:] * piece[8:])
            scaled.append((piece * gain[rows]).astype(BF16))
        squares[:, at : at + NEAR_TILE] = total
        partial[:, at : at + NEAR_TILE] = jnp.dot(
            w_in[:, :near_rows], jnp.concatenate(scaled, 0), preferred_element_type=F32
        ).astype(BF16)


def main_kernel(short_count, block_no, last, *refs):
    nears, pair, far = refs[:6], refs[6], refs[7:12]
    (columns, hidden_columns, w_in, w_out), outs = refs[12:16], refs[16:]
    near_rows, half_rows = nears[0].shape
    local_rows = pair.shape[1]
    width = near_rows + (1 + len(far)) * TRACK_CH
    gain = columns[near_rows:, block_no : block_no + 1]
    b_out = columns[:, BLOCKS + block_no : BLOCKS + block_no + 1]
    b_in = hidden_columns[:, block_no : block_no + 1] * ALPHA
    for begin in range(0, local_rows, TILE):
        end = begin + TILE
        rotated, squares, partial = nears[:3] if begin < half_rows else nears[3:]
        here = slice(begin % half_rows, begin % half_rows + TILE)
        parts = [pair[TRACK_CH:, begin:end].astype(F32)]
        parts += [ref[:TRACK_CH, begin:end].astype(F32) for ref in far]
        total = squares[:, here]
        for part in parts:
            total = total + (part[:8] * part[:8] + part[8:] * part[8:])
        scale = ALPHA * lax.rsqrt(jnp.sum(total, axis=0, keepdims=True) * (1.0 / width) + 1e-06)
        far_part = jnp.concatenate(parts, 0)
        pre = jnp.dot(w_in[:, near_rows:], (far_part * gain).astype(BF16), preferred_element_type=F32)
        pre = (partial[:, here].astype(F32) + pre) * scale + b_in
        inner = pre * (GELU_C + pre * pre)
        active = (pre * (1.0 + jnp.tanh(inner))).astype(BF16)
        out = jnp.dot(w_out[block_no], active, preferred_element_type=F32) * (0.5 / ALPHA) + b_out
        near_out = (rotated[:, here].astype(F32) + out[:near_rows]).astype(BF16)
        far_out = (far_part + out[near_rows:]).astype(BF16)
        outs[0][:near_rows, begin:end] = near_out
        if last:
            outs[0][near_rows:, begin:end] = far_out
        else:
            outs[1][TRACK_CH:, begin:end] = far_out[:TRACK_CH]
            outs[2][:, begin:end] = far_out[TRACK_CH : 3 * TRACK_CH]
            for at in range(3):
                outs[3 + at][:, begin:end] = far_out[(3 + at) * TRACK_CH : (4 + at) * TRACK_CH]
    if not last:

        def track(t, begin, end):
            return outs[0][t * TRACK_CH : (t + 1) * TRACK_CH, begin:end]

        def store(begin, end, value):
            outs[1][:TRACK_CH, begin:end] = value

        pack_halo(track, store, local_rows, short_count)


def call(kernel, out_shape, in_specs, name, limit):
    return pl.pallas_call(
        kernel,
        out_shape=out_shape,
        in_specs=in_specs,
        out_specs=[VMEM] * len(out_shape),
        compiler_params=pltpu.CompilerParams(vmem_limit_bytes=limit << 20),
        cost_estimate=pl.CostEstimate(flops=COST, transcendentals=0, bytes_accessed=COST),
        name=name,
    )


def permuted(value, moves):
    return lax.ppermute(value, "seq", moves)


def routes():
    first, second = [], []
    for y in range(4):
        for z in range(8):
            for x in range(2):
                source = (y * 8 + z) * 2 + x
                middle = (((y + z // 4) % 4) * 8 + (z - 2) % 8) * 2 + x
                first.append((source, middle))
                second.append((middle, (source + 8) % 64))
    return first, second


def exchange(pair, duo, far, fill):
    eight, sixteen, thirty_two = far
    to_middle, from_middle = routes()
    eight = permuted(eight, to_middle)
    duo = shifted(duo, "seq", 2)
    pair = shifted(pair, "seq", 1)
    back = shifted(thirty_two, "seq", -16)
    sixteen = shifted(sixteen, "seq", 16)
    four = shifted(after(duo[TRACK_CH:], eight), "seq", 2)
    back = shifted(after(back, duo), "seq", -16)
    eight = permuted(after(eight, *fill), from_middle)
    return pair, [duo, four, eight, sixteen, back]


def shards(tokens, norm_gain, in_weight, in_bias, out_weight, out_bias):
    width, local_rows = tokens.shape
    half_rows = local_rows // 2
    hidden = in_weight.shape[1]
    short_count = short_tracks(local_rows)
    far_count = TRACKS - 2 - short_count
    near_rows = (1 + short_count) * TRACK_CH
    one = jax.ShapeDtypeStruct((TRACK_CH, local_rows), BF16)
    two = jax.ShapeDtypeStruct((2 * TRACK_CH, local_rows), BF16)
    near_shape = jax.ShapeDtypeStruct((near_rows, local_rows), BF16)
    half_shapes = [
        jax.ShapeDtypeStruct((near_rows, half_rows), BF16),
        jax.ShapeDtypeStruct((8, half_rows), F32),
        jax.ShapeDtypeStruct((hidden, half_rows), BF16),
    ]
    pair, duo, *far = pl.pallas_call(
        functools.partial(first_kernel, short_count),
        out_shape=[two] * 2 + [one] * (far_count - 2),
        in_specs=[pl.BlockSpec(memory_space=pl.ANY)],
        out_specs=[VMEM] * far_count,
        scratch_shapes=[pltpu.VMEM((near_rows, local_rows // 2), BF16)]
        + [pltpu.SemaphoreType.DMA] * (2 + far_count),
        name="first",
    )(tokens)
    made = [((hidden, width), BF16)] * BLOCKS + [((width, 8), F32), ((hidden, 8), F32)]
    *w_ins, columns, hidden_columns = pl.pallas_call(
        weight_kernel,
        out_shape=[jax.ShapeDtypeStruct(*entry) for entry in made],
        in_specs=[VMEM] * 4,
        out_specs=[pl.BlockSpec(memory_space=pltpu.HBM)] * 4,
        scratch_shapes=[pltpu.VMEM(*entry) for entry in made] + [pltpu.SemaphoreType.DMA] * 4,
        name="weights",
    )(jnp.swapaxes(in_weight, 1, 2), in_bias, norm_gain, out_bias)
    near = tokens
    for block_no in range(BLOCKS):
        last = block_no == BLOCKS - 1
        high = call(
            functools.partial(near_kernel, short_count, block_no, half_rows), half_shapes, [VMEM] * 3, "high", 8
        )(near, columns, w_ins[block_no])
        pair, moved = exchange(pair, duo, far, [columns] if block_no == 0 else high[1:2])
        low = call(functools.partial(near_kernel, short_count, block_no, 0), half_shapes, [VMEM] * 4, "low", 8)(
            near, columns, w_ins[block_no], pair
        )
        out_shape = [jax.ShapeDtypeStruct((width, local_rows), BF16)]
        if not last:
            out_shape = [near_shape, two, two] + [one] * (far_count - 2)
        outs = call(
            functools.partial(main_kernel, short_count, block_no, last), out_shape, [VMEM] * 16, "main", 24
        )(*low, *high, pair, *moved, columns, hidden_columns, w_ins[block_no], out_weight)
        if last:
            return outs[0]
        near, pair, duo, far = outs[0], outs[1], outs[2], outs[3:]


def solution(mesh):
    return jax.shard_map(
        shards,
        mesh=mesh,
        in_specs=(P("batch", "seq"), P(), P(), P(), P(), P()),
        out_specs=P("batch", "seq"),
        check_vma=False,
    )
```

```python
import functools

import jax
import jax.numpy as jnp
from jax import lax
from jax.experimental import pallas as pl
from jax.experimental.pallas import tpu as pltpu
from jax.sharding import PartitionSpec as P

TRACK_CH = 16
TRACKS = 19
BLOCKS = 2
LANES = 128
NEAR_TILE = 1024
TILE = 2048
COST = 1
GELU_A = 0.7978845608028654
ALPHA = (GELU_A * 0.044715) ** (1.0 / 3.0)
GELU_C = GELU_A / ALPHA
F32, BF16 = jnp.float32, jnp.bfloat16
VMEM = pl.BlockSpec(memory_space=pltpu.VMEM)


def shifted(value, axis, steps):
    count = lax.axis_size(axis)
    pairs = [(source, (source + steps) % count) for source in range(count)]
    return lax.ppermute(value, axis, pairs)


def after(value, *others):
    return lax.optimization_barrier((value, *others))[0]


def short_tracks(local_rows):
    count = 0
    while count + 1 < TRACKS and 2**count < local_rows:
        count = count + 1
    return count


def pack_halo(track, store, local_rows, short_count):
    lane = lax.broadcasted_iota(jnp.int32, (TRACK_CH, LANES), 1)
    packed = jnp.zeros((TRACK_CH, LANES), F32)
    for slot in range(short_count):
        offset = 2**slot
        if offset < LANES:
            last = track(1 + slot, local_rows - LANES, local_rows).astype(F32)
            moved = pltpu.roll(last, (2 * offset - 1) % LANES, 1)
            inside = (lane >= offset - 1) & (lane < 2 * offset - 1)
            packed = jnp.where(inside, moved, packed)
        else:
            store(offset, 2 * offset, track(1 + slot, local_rows - offset, local_rows))
    store(0, LANES, packed.astype(BF16))


def rotated_piece(track, halo, slot, begin, end):
    offset = 2**slot
    if offset < LANES:
        if begin == 0:
            packed = halo(0, LANES).astype(F32)
            before = pltpu.roll(packed, (LANES + 1 - 2 * offset) % LANES, 1)
            window = jnp.concatenate([before, track(1 + slot, 0, end).astype(F32)], 1)
        else:
            window = track(1 + slot, begin - LANES, end).astype(F32)
        return pltpu.roll(window, offset, 1)[:, LANES:].astype(BF16)
    parts = []
    if begin < offset:
        parts.append(halo(offset + begin, offset + min(end, offset)))
    if end > offset:
        parts.append(track(1 + slot, max(begin, offset) - offset, end - offset))
    return parts[0] if len(parts) == 1 else jnp.concatenate(parts, 1)


def first_kernel(short_count, tokens, *refs):
    pair, duo, far = refs[0], refs[1], refs[2:5]
    tail, sems = refs[5], refs[6:]
    near_rows, half_rows = tail.shape
    local_rows = pair.shape[1]
    base = local_rows - half_rows
    copies = [pltpu.make_async_copy(tokens.at[:near_rows, base:], tail, sems[0])]
    for at, target in enumerate([pair.at[TRACK_CH:, :], duo.at[:TRACK_CH, :], duo.at[TRACK_CH:, :], *far]):
        top = near_rows + at * TRACK_CH
        copies.append(
            pltpu.make_async_copy(tokens.at[top : top + TRACK_CH, :], target, sems[1 + at])
        )
    for copy in copies:
        copy.start()
    copies[0].wait()

    def track(t, begin, end):
        return tail[t * TRACK_CH : (t + 1) * TRACK_CH, begin - base : end - base]

    def store(begin, end, value):
        pair[:TRACK_CH, begin:end] = value

    pack_halo(track, store, local_rows, short_count)
    for copy in copies[1:]:
        copy.wait()


def start_kernel(short_count, half_rows, transposed, bias, gain, last_bias, tokens, *refs):
    outs, high, made, sems = refs[:4], refs[4:7], refs[7:11], refs[11:]
    depth, hidden = transposed.shape[1:]
    copies = []
    for block_no in range(BLOCKS):
        made[block_no][...] = jnp.transpose(transposed[block_no])
        copies.append(pltpu.make_async_copy(made[block_no], outs[block_no], sems[block_no]))
        copies[-1].start()
    columns = [gain[...], last_bias[...], jnp.zeros((8 - 2 * BLOCKS, depth), F32)]
    made[2][...] = jnp.transpose(jnp.concatenate(columns, 0))
    made[3][...] = jnp.transpose(jnp.concatenate([bias[...], jnp.zeros((8 - BLOCKS, hidden), F32)], 0))
    for at in (2, 3):
        copies.append(pltpu.make_async_copy(made[at], outs[at], sems[at]))
        copies[-1].start()
    near_kernel(short_count, 0, half_rows, tokens, made[2], made[0], *high)
    for copy in copies:
        copy.wait()


def near_kernel(short_count, block_no, first, near, columns, w_in, *refs):
    halo_in = refs[0]
    rotated, squares, partial = refs[-3:]
    near_rows, width = rotated.shape
    gain = columns[:near_rows, block_no : block_no + 1]

    def track(t, begin, end):
        return near[t * TRACK_CH : (t + 1) * TRACK_CH, begin:end]

    def halo(begin, end):
        return halo_in[:TRACK_CH, begin:end]

    for at in range(0, width, NEAR_TILE):
        begin, end = first + at, first + at + NEAR_TILE
        total = jnp.zeros((8, NEAR_TILE), F32)
        scaled = []
        for t in range(1 + short_count):
            rows = slice(t * TRACK_CH, (t + 1) * TRACK_CH)
            piece = track(0, begin, end) if t == 0 else rotated_piece(track, halo, t - 1, begin, end)
            rotated[rows, at : at + NEAR_TILE] = piece
            piece = piece.astype(F32)
            total = total + (piece[:8] * piece[:8] + piece[8:] * piece[8:])
            scaled.append((piece * gain[rows]).astype(BF16))
        squares[:, at : at + NEAR_TILE] = total
        partial[:, at : at + NEAR_TILE] = jnp.dot(
            w_in[:, :near_rows], jnp.concatenate(scaled, 0), preferred_element_type=F32
        ).astype(BF16)


def main_kernel(short_count, block_no, last, *refs):
    nears, pair, far = refs[:6], refs[6], refs[7:12]
    (columns, hidden_columns, w_in, w_out), outs = refs[12:16], refs[16:]
    copies = []
    near_rows, half_rows = nears[0].shape
    local_rows = pair.shape[1]
    width = near_rows + (1 + len(far)) * TRACK_CH
    gain = columns[near_rows:, block_no : block_no + 1]
    b_out = columns[:, BLOCKS + block_no : BLOCKS + block_no + 1]
    b_in = hidden_columns[:, block_no : block_no + 1] * ALPHA
    for begin in range(0, local_rows, TILE):
        end = begin + TILE
        rotated, squares, partial = nears[:3] if begin < half_rows else nears[3:]
        here = slice(begin % half_rows, begin % half_rows + TILE)
        parts = [pair[TRACK_CH:, begin:end].astype(F32)]
        parts += [ref[:TRACK_CH, begin:end].astype(F32) for ref in far]
        total = squares[:, here]
        for part in parts:
            total = total + (part[:8] * part[:8] + part[8:] * part[8:])
        scale = ALPHA * lax.rsqrt(jnp.sum(total, axis=0, keepdims=True) * (1.0 / width) + 1e-06)
        far_part = jnp.concatenate(parts, 0)
        pre = jnp.dot(w_in[:, near_rows:], (far_part * gain).astype(BF16), preferred_element_type=F32)
        pre = (partial[:, here].astype(F32) + pre) * scale + b_in
        inner = pre * (GELU_C + pre * pre)
        active = (pre * (1.0 + jnp.tanh(inner))).astype(BF16)
        out = jnp.dot(w_out[block_no], active, preferred_element_type=F32) * (0.5 / ALPHA) + b_out
        near_out = (rotated[:, here].astype(F32) + out[:near_rows]).astype(BF16)
        far_out = (far_part + out[near_rows:]).astype(BF16)
        if last:
            made = outs[1]
            made[:near_rows, begin:end] = near_out
            made[near_rows:, begin:end] = far_out
            copy = pltpu.make_async_copy(
                made.at[:, begin:end], outs[0].at[:, begin:end], outs[2 + len(copies)]
            )
            copy.start()
            copies.append(copy)
        else:
            outs[0][:, begin:end] = near_out
            outs[1][TRACK_CH:, begin:end] = far_out[:TRACK_CH]
            outs[2][:, begin:end] = far_out[TRACK_CH : 3 * TRACK_CH]
            for at in range(3):
                outs[3 + at][:, begin:end] = far_out[(3 + at) * TRACK_CH : (4 + at) * TRACK_CH]
    for copy in copies:
        copy.wait()
    if not last:

        def track(t, begin, end):
            return outs[0][t * TRACK_CH : (t + 1) * TRACK_CH, begin:end]

        def store(begin, end, value):
            outs[1][:TRACK_CH, begin:end] = value

        pack_halo(track, store, local_rows, short_count)


def call(kernel, out_shape, in_specs, name, limit, out_specs=None, scratch=()):
    return pl.pallas_call(
        kernel,
        out_shape=out_shape,
        in_specs=in_specs,
        out_specs=out_specs or [VMEM] * len(out_shape),
        scratch_shapes=scratch,
        compiler_params=pltpu.CompilerParams(vmem_limit_bytes=limit << 20),
        cost_estimate=pl.CostEstimate(flops=COST, transcendentals=0, bytes_accessed=COST),
        name=name,
    )


def permuted(value, moves):
    return lax.ppermute(value, "seq", moves)


def routes():
    first, second = [], []
    for y in range(4):
        for z in range(8):
            for x in range(2):
                source = (y * 8 + z) * 2 + x
                middle = (((y + z // 4) % 4) * 8 + (z - 2) % 8) * 2 + x
                first.append((source, middle))
                second.append((middle, (source + 8) % 64))
    return first, second


def exchange(pair, duo, far, fill):
    eight, sixteen, thirty_two = far
    to_middle, from_middle = routes()
    eight = permuted(eight, to_middle)
    duo = shifted(duo, "seq", 2)
    pair = shifted(pair, "seq", 1)
    back = shifted(thirty_two, "seq", -16)
    sixteen = shifted(sixteen, "seq", 16)
    four = shifted(after(duo[TRACK_CH:], eight), "seq", 2)
    back = shifted(after(back, duo), "seq", -16)
    eight = permuted(after(eight, *fill), from_middle)
    return pair, [duo, four, eight, sixteen, back]


def shards(tokens, norm_gain, in_weight, in_bias, out_weight, out_bias):
    width, local_rows = tokens.shape
    half_rows = local_rows // 2
    hidden = in_weight.shape[1]
    short_count = short_tracks(local_rows)
    far_count = TRACKS - 2 - short_count
    near_rows = (1 + short_count) * TRACK_CH
    one = jax.ShapeDtypeStruct((TRACK_CH, local_rows), BF16)
    two = jax.ShapeDtypeStruct((2 * TRACK_CH, local_rows), BF16)
    near_shape = jax.ShapeDtypeStruct((near_rows, local_rows), BF16)
    half_shapes = [
        jax.ShapeDtypeStruct((near_rows, half_rows), BF16),
        jax.ShapeDtypeStruct((8, half_rows), F32),
        jax.ShapeDtypeStruct((hidden, half_rows), BF16),
    ]
    pair, duo, *far = pl.pallas_call(
        functools.partial(first_kernel, short_count),
        out_shape=[two] * 2 + [one] * (far_count - 2),
        in_specs=[pl.BlockSpec(memory_space=pl.ANY)],
        out_specs=[VMEM] * far_count,
        scratch_shapes=[pltpu.VMEM((near_rows, local_rows // 2), BF16)]
        + [pltpu.SemaphoreType.DMA] * (2 + far_count),
        name="first",
    )(tokens)
    made = [((hidden, width), BF16)] * BLOCKS + [((width, 8), F32), ((hidden, 8), F32)]
    *w_ins, columns, hidden_columns, rotated, squares, partial = pl.pallas_call(
        functools.partial(start_kernel, short_count, half_rows),
        out_shape=[jax.ShapeDtypeStruct(*entry) for entry in made] + half_shapes,
        in_specs=[VMEM] * 5,
        out_specs=[pl.BlockSpec(memory_space=pltpu.HBM)] * 4 + [VMEM] * 3,
        scratch_shapes=[pltpu.VMEM(*entry) for entry in made] + [pltpu.SemaphoreType.DMA] * 4,
        compiler_params=pltpu.CompilerParams(vmem_limit_bytes=16 << 20),
        name="start",
    )(jnp.swapaxes(in_weight, 1, 2), in_bias, norm_gain, out_bias, tokens)
    high = [rotated, squares, partial]
    near = tokens
    for block_no in range(BLOCKS):
        last = block_no == BLOCKS - 1
        if block_no:
            high = call(
                functools.partial(near_kernel, short_count, block_no, half_rows), half_shapes, [VMEM] * 3, "high", 8
            )(near, columns, w_ins[block_no])
        pair, moved = exchange(pair, duo, far, [high[1]])
        low = call(functools.partial(near_kernel, short_count, block_no, 0), half_shapes, [VMEM] * 4, "low", 8)(
            near, columns, w_ins[block_no], pair
        )
        out_shape = [jax.ShapeDtypeStruct((width, local_rows), BF16)]
        if not last:
            out_shape = [near_shape, two, two] + [one] * (far_count - 2)
        out_specs, scratch = [VMEM] * len(out_shape), []
        if last:
            out_specs = [pl.BlockSpec(memory_space=pltpu.HBM)]
            scratch = [pltpu.VMEM((width, local_rows), BF16)] + [pltpu.SemaphoreType.DMA] * (local_rows // TILE)
        outs = call(
            functools.partial(main_kernel, short_count, block_no, last), out_shape, [VMEM] * 16, "main", 24, out_specs, scratch
        )(*low, *high, pair, *moved, columns, hidden_columns, w_ins[block_no], out_weight)
        if last:
            return outs[0]
        near, pair, duo, far = outs[0], outs[1], outs[2], outs[3:]


def solution(mesh):
    return jax.shard_map(
        shards,
        mesh=mesh,
        in_specs=(P("batch", "seq"), P(), P(), P(), P(), P()),
        out_specs=P("batch", "seq"),
        check_vma=False,
    )
```

```python
import functools

import jax
import jax.numpy as jnp
from jax import lax
from jax.experimental import pallas as pl
from jax.experimental.pallas import tpu as pltpu
from jax.sharding import PartitionSpec as P

TRACK_CH = 16
TRACKS = 19
BLOCKS = 2
LANES = 128
NEAR_TILE = 1024
TILE = 2048
LAST_TILE = 1024
COST = 1
GELU_A = 0.7978845608028654
ALPHA = (GELU_A * 0.044715) ** (1.0 / 3.0)
GELU_C = GELU_A / ALPHA
F32, BF16 = jnp.float32, jnp.bfloat16
VMEM = pl.BlockSpec(memory_space=pltpu.VMEM)


def shifted(value, axis, steps):
    count = lax.axis_size(axis)
    pairs = [(source, (source + steps) % count) for source in range(count)]
    return lax.ppermute(value, axis, pairs)


def after(value, *others):
    return lax.optimization_barrier((value, *others))[0]


def short_tracks(local_rows):
    count = 0
    while count + 1 < TRACKS and 2**count < local_rows:
        count = count + 1
    return count


def pack_halo(track, store, local_rows, short_count):
    lane = lax.broadcasted_iota(jnp.int32, (TRACK_CH, LANES), 1)
    packed = jnp.zeros((TRACK_CH, LANES), F32)
    for slot in range(short_count):
        offset = 2**slot
        if offset < LANES:
            last = track(1 + slot, local_rows - LANES, local_rows).astype(F32)
            moved = pltpu.roll(last, (2 * offset - 1) % LANES, 1)
            inside = (lane >= offset - 1) & (lane < 2 * offset - 1)
            packed = jnp.where(inside, moved, packed)
        else:
            store(offset, 2 * offset, track(1 + slot, local_rows - offset, local_rows))
    store(0, LANES, packed.astype(BF16))


def rotated_piece(track, halo, slot, begin, end):
    offset = 2**slot
    if offset < LANES:
        if begin == 0:
            packed = halo(0, LANES).astype(F32)
            before = pltpu.roll(packed, (LANES + 1 - 2 * offset) % LANES, 1)
            window = jnp.concatenate([before, track(1 + slot, 0, end).astype(F32)], 1)
        else:
            window = track(1 + slot, begin - LANES, end).astype(F32)
        return pltpu.roll(window, offset, 1)[:, LANES:].astype(BF16)
    parts = []
    if begin < offset:
        parts.append(halo(offset + begin, offset + min(end, offset)))
    if end > offset:
        parts.append(track(1 + slot, max(begin, offset) - offset, end - offset))
    return parts[0] if len(parts) == 1 else jnp.concatenate(parts, 1)


def first_kernel(short_count, tokens, *refs):
    pair, duo, far = refs[0], refs[1], refs[2:5]
    tail, sems = refs[5], refs[6:]
    near_rows, half_rows = tail.shape
    local_rows = pair.shape[1]
    base = local_rows - half_rows
    copies = [pltpu.make_async_copy(tokens.at[:near_rows, base:], tail, sems[0])]
    for at, target in enumerate([pair.at[TRACK_CH:, :], duo.at[:TRACK_CH, :], duo.at[TRACK_CH:, :], *far]):
        top = near_rows + at * TRACK_CH
        copies.append(
            pltpu.make_async_copy(tokens.at[top : top + TRACK_CH, :], target, sems[1 + at])
        )
    for copy in copies:
        copy.start()
    copies[0].wait()

    def track(t, begin, end):
        return tail[t * TRACK_CH : (t + 1) * TRACK_CH, begin - base : end - base]

    def store(begin, end, value):
        pair[:TRACK_CH, begin:end] = value

    pack_halo(track, store, local_rows, short_count)
    for copy in copies[1:]:
        copy.wait()


def start_kernel(short_count, half_rows, transposed, bias, gain, last_bias, tokens, *refs):
    outs, high, made, sems = refs[:4], refs[4:7], refs[7:11], refs[11:]
    depth, hidden = transposed.shape[1:]
    copies = []
    for block_no in range(BLOCKS):
        made[block_no][...] = jnp.transpose(transposed[block_no])
        copies.append(pltpu.make_async_copy(made[block_no], outs[block_no], sems[block_no]))
        copies[-1].start()
    columns = [gain[...], last_bias[...], jnp.zeros((8 - 2 * BLOCKS, depth), F32)]
    made[2][...] = jnp.transpose(jnp.concatenate(columns, 0))
    made[3][...] = jnp.transpose(jnp.concatenate([bias[...], jnp.zeros((8 - BLOCKS, hidden), F32)], 0))
    for at in (2, 3):
        copies.append(pltpu.make_async_copy(made[at], outs[at], sems[at]))
        copies[-1].start()
    near_kernel(short_count, 0, half_rows, tokens, made[2], made[0], *high)
    for copy in copies:
        copy.wait()


def near_kernel(short_count, block_no, first, near, columns, w_in, *refs):
    halo_in = refs[0]
    rotated, squares, partial = refs[-3:]
    near_rows, width = rotated.shape
    gain = columns[:near_rows, block_no : block_no + 1]

    def track(t, begin, end):
        return near[t * TRACK_CH : (t + 1) * TRACK_CH, begin:end]

    def halo(begin, end):
        return halo_in[:TRACK_CH, begin:end]

    for at in range(0, width, NEAR_TILE):
        begin, end = first + at, first + at + NEAR_TILE
        total = jnp.zeros((8, NEAR_TILE), F32)
        scaled = []
        for t in range(1 + short_count):
            rows = slice(t * TRACK_CH, (t + 1) * TRACK_CH)
            piece = track(0, begin, end) if t == 0 else rotated_piece(track, halo, t - 1, begin, end)
            rotated[rows, at : at + NEAR_TILE] = piece
            piece = piece.astype(F32)
            total = total + (piece[:8] * piece[:8] + piece[8:] * piece[8:])
            scaled.append((piece * gain[rows]).astype(BF16))
        squares[:, at : at + NEAR_TILE] = total
        partial[:, at : at + NEAR_TILE] = jnp.dot(
            w_in[:, :near_rows], jnp.concatenate(scaled, 0), preferred_element_type=F32
        ).astype(BF16)


def main_kernel(short_count, block_no, last, *refs):
    nears, pair, far = refs[:6], refs[6], refs[7:12]
    (columns, hidden_columns, w_in, w_out), outs = refs[12:16], refs[16:]
    copies = []
    near_rows, half_rows = nears[0].shape
    local_rows = pair.shape[1]
    width = near_rows + (1 + len(far)) * TRACK_CH
    gain = columns[near_rows:, block_no : block_no + 1]
    b_out = columns[:, BLOCKS + block_no : BLOCKS + block_no + 1]
    b_in = hidden_columns[:, block_no : block_no + 1] * ALPHA
    tile = LAST_TILE if last else TILE
    for begin in range(0, local_rows, tile):
        end = begin + tile
        rotated, squares, partial = nears[:3] if begin < half_rows else nears[3:]
        here = slice(begin % half_rows, begin % half_rows + tile)
        parts = [pair[TRACK_CH:, begin:end].astype(F32)]
        parts += [ref[:TRACK_CH, begin:end].astype(F32) for ref in far]
        total = squares[:, here]
        for part in parts:
            total = total + (part[:8] * part[:8] + part[8:] * part[8:])
        scale = ALPHA * lax.rsqrt(jnp.sum(total, axis=0, keepdims=True) * (1.0 / width) + 1e-06)
        far_part = jnp.concatenate(parts, 0)
        pre = jnp.dot(w_in[:, near_rows:], (far_part * gain).astype(BF16), preferred_element_type=F32)
        pre = (partial[:, here].astype(F32) + pre) * scale + b_in
        inner = pre * (GELU_C + pre * pre)
        active = (pre * (1.0 + jnp.tanh(inner))).astype(BF16)
        out = jnp.dot(w_out[block_no], active, preferred_element_type=F32) * (0.5 / ALPHA) + b_out
        near_out = (rotated[:, here].astype(F32) + out[:near_rows]).astype(BF16)
        far_out = (far_part + out[near_rows:]).astype(BF16)
        if last:
            made = outs[1]
            made[:near_rows, begin:end] = near_out
            made[near_rows:, begin:end] = far_out
            copy = pltpu.make_async_copy(
                made.at[:, begin:end], outs[0].at[:, begin:end], outs[2 + len(copies)]
            )
            copy.start()
            copies.append(copy)
        else:
            outs[0][:, begin:end] = near_out
            outs[1][TRACK_CH:, begin:end] = far_out[:TRACK_CH]
            outs[2][:, begin:end] = far_out[TRACK_CH : 3 * TRACK_CH]
            for at in range(3):
                outs[3 + at][:, begin:end] = far_out[(3 + at) * TRACK_CH : (4 + at) * TRACK_CH]
    for copy in copies:
        copy.wait()
    if not last:

        def track(t, begin, end):
            return outs[0][t * TRACK_CH : (t + 1) * TRACK_CH, begin:end]

        def store(begin, end, value):
            outs[1][:TRACK_CH, begin:end] = value

        pack_halo(track, store, local_rows, short_count)


def call(kernel, out_shape, in_specs, name, limit, out_specs=None, scratch=()):
    return pl.pallas_call(
        kernel,
        out_shape=out_shape,
        in_specs=in_specs,
        out_specs=out_specs or [VMEM] * len(out_shape),
        scratch_shapes=scratch,
        compiler_params=pltpu.CompilerParams(vmem_limit_bytes=limit << 20),
        cost_estimate=pl.CostEstimate(flops=COST, transcendentals=0, bytes_accessed=COST),
        name=name,
    )


def permuted(value, moves):
    return lax.ppermute(value, "seq", moves)


def routes():
    first, second = [], []
    for y in range(4):
        for z in range(8):
            for x in range(2):
                source = (y * 8 + z) * 2 + x
                middle = (((y + z // 4) % 4) * 8 + (z - 2) % 8) * 2 + x
                first.append((source, middle))
                second.append((middle, (source + 8) % 64))
    return first, second


def exchange(pair, duo, far, fill):
    eight, sixteen, thirty_two = far
    to_middle, from_middle = routes()
    eight = permuted(eight, to_middle)
    duo = shifted(duo, "seq", 2)
    pair = shifted(pair, "seq", 1)
    back = shifted(thirty_two, "seq", 32)
    sixteen = shifted(sixteen, "seq", 16)
    four = shifted(after(duo[TRACK_CH:], eight), "seq", 2)
    eight = permuted(after(eight, *fill), from_middle)
    return pair, [duo, four, eight, sixteen, back]


def shards(tokens, norm_gain, in_weight, in_bias, out_weight, out_bias):
    width, local_rows = tokens.shape
    half_rows = local_rows // 2
    hidden = in_weight.shape[1]
    short_count = short_tracks(local_rows)
    far_count = TRACKS - 2 - short_count
    near_rows = (1 + short_count) * TRACK_CH
    one = jax.ShapeDtypeStruct((TRACK_CH, local_rows), BF16)
    two = jax.ShapeDtypeStruct((2 * TRACK_CH, local_rows), BF16)
    near_shape = jax.ShapeDtypeStruct((near_rows, local_rows), BF16)
    half_shapes = [
        jax.ShapeDtypeStruct((near_rows, half_rows), BF16),
        jax.ShapeDtypeStruct((8, half_rows), F32),
        jax.ShapeDtypeStruct((hidden, half_rows), BF16),
    ]
    pair, duo, *far = pl.pallas_call(
        functools.partial(first_kernel, short_count),
        out_shape=[two] * 2 + [one] * (far_count - 2),
        in_specs=[pl.BlockSpec(memory_space=pl.ANY)],
        out_specs=[VMEM] * far_count,
        scratch_shapes=[pltpu.VMEM((near_rows, local_rows // 2), BF16)]
        + [pltpu.SemaphoreType.DMA] * (2 + far_count),
        name="first",
    )(tokens)
    made = [((hidden, width), BF16)] * BLOCKS + [((width, 8), F32), ((hidden, 8), F32)]
    *w_ins, columns, hidden_columns, rotated, squares, partial = pl.pallas_call(
        functools.partial(start_kernel, short_count, half_rows),
        out_shape=[jax.ShapeDtypeStruct(*entry) for entry in made] + half_shapes,
        in_specs=[VMEM] * 5,
        out_specs=[pl.BlockSpec(memory_space=pltpu.HBM)] * 4 + [VMEM] * 3,
        scratch_shapes=[pltpu.VMEM(*entry) for entry in made] + [pltpu.SemaphoreType.DMA] * 4,
        compiler_params=pltpu.CompilerParams(vmem_limit_bytes=16 << 20),
        name="start",
    )(jnp.swapaxes(in_weight, 1, 2), in_bias, norm_gain, out_bias, tokens)
    high = [rotated, squares, partial]
    near = tokens
    for block_no in range(BLOCKS):
        last = block_no == BLOCKS - 1
        if block_no:
            high = call(
                functools.partial(near_kernel, short_count, block_no, half_rows), half_shapes, [VMEM] * 3, "high", 8
            )(near, columns, w_ins[block_no])
        pair, moved = exchange(pair, duo, far, [high[1]])
        low = call(functools.partial(near_kernel, short_count, block_no, 0), half_shapes, [VMEM] * 4, "low", 8)(
            near, columns, w_ins[block_no], pair
        )
        out_shape = [jax.ShapeDtypeStruct((width, local_rows), BF16)]
        if not last:
            out_shape = [near_shape, two, two] + [one] * (far_count - 2)
        out_specs, scratch = [VMEM] * len(out_shape), []
        if last:
            out_specs = [pl.BlockSpec(memory_space=pltpu.HBM)]
            scratch = [pltpu.VMEM((width, local_rows), BF16)] + [pltpu.SemaphoreType.DMA] * (local_rows // LAST_TILE)
        outs = call(
            functools.partial(main_kernel, short_count, block_no, last), out_shape, [VMEM] * 16, "main", 24, out_specs, scratch
        )(*low, *high, pair, *moved, columns, hidden_columns, w_ins[block_no], out_weight)
        if last:
            return outs[0]
        near, pair, duo, far = outs[0], outs[1], outs[2], outs[3:]


def solution(mesh):
    return jax.shard_map(
        shards,
        mesh=mesh,
        in_specs=(P("batch", "seq"), P(), P(), P(), P(), P()),
        out_specs=P("batch", "seq"),
        check_vma=False,
    )
```

```python
import functools

import jax
import jax.numpy as jnp
from jax import lax
from jax.experimental import pallas as pl
from jax.experimental.pallas import tpu as pltpu
from jax.sharding import PartitionSpec as P

TRACK_CH = 16
TRACKS = 19
BLOCKS = 2
LANES = 128
NEAR_TILE = 1024
TILE = 2048
LAST_TILE = 1024
COST = 1
GELU_A = 0.7978845608028654
ALPHA = (GELU_A * 0.044715) ** (1.0 / 3.0)
GELU_C = GELU_A / ALPHA
F32, BF16 = jnp.float32, jnp.bfloat16
VMEM = pl.BlockSpec(memory_space=pltpu.VMEM)


def shifted(value, axis, steps):
    count = lax.axis_size(axis)
    pairs = [(source, (source + steps) % count) for source in range(count)]
    return lax.ppermute(value, axis, pairs)


def after(value, *others):
    return lax.optimization_barrier((value, *others))[0]


def short_tracks(local_rows):
    count = 0
    while count + 1 < TRACKS and 2**count < local_rows:
        count = count + 1
    return count


def pack_halo(track, store, local_rows, short_count):
    lane = lax.broadcasted_iota(jnp.int32, (TRACK_CH, LANES), 1)
    packed = jnp.zeros((TRACK_CH, LANES), F32)
    for slot in range(short_count):
        offset = 2**slot
        if offset < LANES:
            last = track(1 + slot, local_rows - LANES, local_rows).astype(F32)
            moved = pltpu.roll(last, (2 * offset - 1) % LANES, 1)
            inside = (lane >= offset - 1) & (lane < 2 * offset - 1)
            packed = jnp.where(inside, moved, packed)
        else:
            store(offset, 2 * offset, track(1 + slot, local_rows - offset, local_rows))
    store(0, LANES, packed.astype(BF16))


def rotated_piece(track, halo, slot, begin, end):
    offset = 2**slot
    if offset < LANES:
        if begin == 0:
            packed = halo(0, LANES).astype(F32)
            before = pltpu.roll(packed, (LANES + 1 - 2 * offset) % LANES, 1)
            window = jnp.concatenate([before, track(1 + slot, 0, end).astype(F32)], 1)
        else:
            window = track(1 + slot, begin - LANES, end).astype(F32)
        return pltpu.roll(window, offset, 1)[:, LANES:].astype(BF16)
    parts = []
    if begin < offset:
        parts.append(halo(offset + begin, offset + min(end, offset)))
    if end > offset:
        parts.append(track(1 + slot, max(begin, offset) - offset, end - offset))
    return parts[0] if len(parts) == 1 else jnp.concatenate(parts, 1)


def first_kernel(short_count, tokens, *refs):
    pair, duo, far = refs[0], refs[1], refs[2:5]
    tail, sems = refs[5], refs[6:]
    near_rows, half_rows = tail.shape
    local_rows = pair.shape[1]
    base = local_rows - half_rows
    copies = [pltpu.make_async_copy(tokens.at[:near_rows, base:], tail, sems[0])]
    for at, target in enumerate([pair.at[TRACK_CH:, :], duo.at[:TRACK_CH, :], duo.at[TRACK_CH:, :], *far]):
        top = near_rows + at * TRACK_CH
        copies.append(
            pltpu.make_async_copy(tokens.at[top : top + TRACK_CH, :], target, sems[1 + at])
        )
    for copy in copies:
        copy.start()
    copies[0].wait()

    def track(t, begin, end):
        return tail[t * TRACK_CH : (t + 1) * TRACK_CH, begin - base : end - base]

    def store(begin, end, value):
        pair[:TRACK_CH, begin:end] = value

    pack_halo(track, store, local_rows, short_count)
    for copy in copies[1:]:
        copy.wait()


def start_kernel(short_count, half_rows, transposed, bias, gain, last_bias, tokens, *refs):
    outs, high, made, sems = refs[:4], refs[4:7], refs[7:11], refs[11:15]
    loaded, load_sems = refs[15:17], refs[17:19]
    depth, hidden = transposed.shape[1:]
    loads, copies = [], []
    for block_no in range(BLOCKS):
        loads.append(pltpu.make_async_copy(transposed.at[block_no], loaded[block_no], load_sems[block_no]))
        loads[-1].start()

    def send(at):
        copies.append(pltpu.make_async_copy(made[at], outs[at], sems[at]))
        copies[-1].start()

    columns = [gain[...], last_bias[...], jnp.zeros((8 - 2 * BLOCKS, depth), F32)]
    made[2][...] = jnp.transpose(jnp.concatenate(columns, 0))
    made[3][...] = jnp.transpose(jnp.concatenate([bias[...], jnp.zeros((8 - BLOCKS, hidden), F32)], 0))
    send(2)
    send(3)
    near_rotate(short_count, half_rows, tokens, None, high[0], high[1])
    for block_no in range(BLOCKS):
        loads[block_no].wait()
        made[block_no][...] = jnp.transpose(loaded[block_no][...])
        send(block_no)
        if block_no == 0:
            near_product(0, made[2], made[0], high[0], high[2])
    for copy in copies:
        copy.wait()


def near_rotate(short_count, first, near, halo_in, rotated, squares):
    width = rotated.shape[1]

    def track(t, begin, end):
        return near[t * TRACK_CH : (t + 1) * TRACK_CH, begin:end]

    def halo(begin, end):
        return halo_in[:TRACK_CH, begin:end]

    for at in range(0, width, NEAR_TILE):
        begin, end = first + at, first + at + NEAR_TILE
        total = jnp.zeros((8, NEAR_TILE), F32)
        for t in range(1 + short_count):
            piece = track(0, begin, end) if t == 0 else rotated_piece(track, halo, t - 1, begin, end)
            rotated[t * TRACK_CH : (t + 1) * TRACK_CH, at : at + NEAR_TILE] = piece
            piece = piece.astype(F32)
            total = total + (piece[:8] * piece[:8] + piece[8:] * piece[8:])
        squares[:, at : at + NEAR_TILE] = total


def near_product(block_no, columns, w_in, rotated, partial):
    near_rows, width = rotated.shape
    gain = columns[:near_rows, block_no : block_no + 1]
    for at in range(0, width, NEAR_TILE):
        here = slice(at, at + NEAR_TILE)
        scaled = (rotated[:, here].astype(F32) * gain).astype(BF16)
        partial[:, here] = jnp.dot(w_in[:, :near_rows], scaled, preferred_element_type=F32).astype(BF16)


def near_kernel(short_count, block_no, first, near, columns, w_in, *refs):
    rotated, squares, partial = refs[-3:]
    near_rotate(short_count, first, near, refs[0], rotated, squares)
    near_product(block_no, columns, w_in, rotated, partial)


def main_kernel(short_count, block_no, last, *refs):
    nears, pair, far = refs[:6], refs[6], refs[7:12]
    (columns, hidden_columns, w_in, w_out), outs = refs[12:16], refs[16:]
    copies = []
    near_rows, half_rows = nears[0].shape
    local_rows = pair.shape[1]
    width = near_rows + (1 + len(far)) * TRACK_CH
    gain = columns[near_rows:, block_no : block_no + 1]
    b_out = columns[:, BLOCKS + block_no : BLOCKS + block_no + 1]
    b_in = hidden_columns[:, block_no : block_no + 1] * ALPHA
    tile = LAST_TILE if last else TILE
    for begin in range(0, local_rows, tile):
        end = begin + tile
        rotated, squares, partial = nears[:3] if begin < half_rows else nears[3:]
        here = slice(begin % half_rows, begin % half_rows + tile)
        parts = [pair[TRACK_CH:, begin:end].astype(F32)]
        parts += [ref[:TRACK_CH, begin:end].astype(F32) for ref in far]
        total = squares[:, here]
        for part in parts:
            total = total + (part[:8] * part[:8] + part[8:] * part[8:])
        scale = ALPHA * lax.rsqrt(jnp.sum(total, axis=0, keepdims=True) * (1.0 / width) + 1e-06)
        far_part = jnp.concatenate(parts, 0)
        pre = jnp.dot(w_in[:, near_rows:], (far_part * gain).astype(BF16), preferred_element_type=F32)
        pre = (partial[:, here].astype(F32) + pre) * scale + b_in
        inner = pre * (GELU_C + pre * pre)
        active = (pre * (1.0 + jnp.tanh(inner))).astype(BF16)
        out = jnp.dot(w_out[block_no], active, preferred_element_type=F32) * (0.5 / ALPHA) + b_out
        near_out = (rotated[:, here].astype(F32) + out[:near_rows]).astype(BF16)
        far_out = (far_part + out[near_rows:]).astype(BF16)
        if last:
            made = outs[1]
            made[:near_rows, begin:end] = near_out
            made[near_rows:, begin:end] = far_out
            copy = pltpu.make_async_copy(
                made.at[:, begin:end], outs[0].at[:, begin:end], outs[2 + len(copies)]
            )
            copy.start()
            copies.append(copy)
        else:
            outs[0][:, begin:end] = near_out
            outs[1][TRACK_CH:, begin:end] = far_out[:TRACK_CH]
            outs[2][:, begin:end] = far_out[TRACK_CH : 3 * TRACK_CH]
            for at in range(3):
                outs[3 + at][:, begin:end] = far_out[(3 + at) * TRACK_CH : (4 + at) * TRACK_CH]
    for copy in copies:
        copy.wait()
    if not last:

        def track(t, begin, end):
            return outs[0][t * TRACK_CH : (t + 1) * TRACK_CH, begin:end]

        def store(begin, end, value):
            outs[1][:TRACK_CH, begin:end] = value

        pack_halo(track, store, local_rows, short_count)


def call(kernel, out_shape, in_specs, name, limit, out_specs=None, scratch=()):
    return pl.pallas_call(
        kernel,
        out_shape=out_shape,
        in_specs=in_specs,
        out_specs=out_specs or [VMEM] * len(out_shape),
        scratch_shapes=scratch,
        compiler_params=pltpu.CompilerParams(vmem_limit_bytes=limit << 20),
        cost_estimate=pl.CostEstimate(flops=COST, transcendentals=0, bytes_accessed=COST),
        name=name,
    )


def permuted(value, moves):
    return lax.ppermute(value, "seq", moves)


def routes():
    first, second = [], []
    for y in range(4):
        for z in range(8):
            for x in range(2):
                source = (y * 8 + z) * 2 + x
                middle = (((y + z // 4) % 4) * 8 + (z - 2) % 8) * 2 + x
                first.append((source, middle))
                second.append((middle, (source + 8) % 64))
    return first, second


def exchange(pair, duo, far, fill):
    eight, sixteen, thirty_two = far
    to_middle, from_middle = routes()
    eight = permuted(eight, to_middle)
    duo = shifted(duo, "seq", 2)
    pair = shifted(pair, "seq", 1)
    back = shifted(thirty_two, "seq", -16)
    sixteen = shifted(sixteen, "seq", 16)
    four = shifted(after(duo[TRACK_CH:], eight), "seq", 2)
    back = shifted(after(back, duo), "seq", -16)
    eight = permuted(after(eight, *fill), from_middle)
    return pair, [duo, four, eight, sixteen, back]


def shards(tokens, norm_gain, in_weight, in_bias, out_weight, out_bias):
    width, local_rows = tokens.shape
    half_rows = local_rows // 2
    hidden = in_weight.shape[1]
    short_count = short_tracks(local_rows)
    far_count = TRACKS - 2 - short_count
    near_rows = (1 + short_count) * TRACK_CH
    one = jax.ShapeDtypeStruct((TRACK_CH, local_rows), BF16)
    two = jax.ShapeDtypeStruct((2 * TRACK_CH, local_rows), BF16)
    near_shape = jax.ShapeDtypeStruct((near_rows, local_rows), BF16)
    half_shapes = [
        jax.ShapeDtypeStruct((near_rows, half_rows), BF16),
        jax.ShapeDtypeStruct((8, half_rows), F32),
        jax.ShapeDtypeStruct((hidden, half_rows), BF16),
    ]
    pair, duo, *far = pl.pallas_call(
        functools.partial(first_kernel, short_count),
        out_shape=[two] * 2 + [one] * (far_count - 2),
        in_specs=[pl.BlockSpec(memory_space=pl.ANY)],
        out_specs=[VMEM] * far_count,
        scratch_shapes=[pltpu.VMEM((near_rows, local_rows // 2), BF16)]
        + [pltpu.SemaphoreType.DMA] * (2 + far_count),
        name="first",
    )(tokens)
    made = [((hidden, width), BF16)] * BLOCKS + [((width, 8), F32), ((hidden, 8), F32)]
    *w_ins, columns, hidden_columns, rotated, squares, partial = pl.pallas_call(
        functools.partial(start_kernel, short_count, half_rows),
        out_shape=[jax.ShapeDtypeStruct(*entry) for entry in made] + half_shapes,
        in_specs=[pl.BlockSpec(memory_space=pltpu.HBM)] + [VMEM] * 4,
        out_specs=[pl.BlockSpec(memory_space=pltpu.HBM)] * 4 + [VMEM] * 3,
        scratch_shapes=[pltpu.VMEM(*entry) for entry in made]
        + [pltpu.SemaphoreType.DMA] * 4
        + [pltpu.VMEM((width, hidden), BF16)] * BLOCKS
        + [pltpu.SemaphoreType.DMA] * BLOCKS,
        compiler_params=pltpu.CompilerParams(vmem_limit_bytes=16 << 20),
        name="start",
    )(pltpu.with_memory_space_constraint(jnp.swapaxes(in_weight, 1, 2), pltpu.HBM), in_bias, norm_gain, out_bias, tokens)
    high = [rotated, squares, partial]
    near = tokens
    for block_no in range(BLOCKS):
        last = block_no == BLOCKS - 1
        if block_no:
            high = call(
                functools.partial(near_kernel, short_count, block_no, half_rows), half_shapes, [VMEM] * 3, "high", 8
            )(near, columns, w_ins[block_no])
        pair, moved = exchange(pair, duo, far, [high[1]])
        low = call(functools.partial(near_kernel, short_count, block_no, 0), half_shapes, [VMEM] * 4, "low", 8)(
            near, columns, w_ins[block_no], pair
        )
        out_shape = [jax.ShapeDtypeStruct((width, local_rows), BF16)]
        if not last:
            out_shape = [near_shape, two, two] + [one] * (far_count - 2)
        out_specs, scratch = [VMEM] * len(out_shape), []
        if last:
            out_specs = [pl.BlockSpec(memory_space=pltpu.HBM)]
            scratch = [pltpu.VMEM((width, local_rows), BF16)] + [pltpu.SemaphoreType.DMA] * (local_rows // LAST_TILE)
        outs = call(
            functools.partial(main_kernel, short_count, block_no, last), out_shape, [VMEM] * 16, "main", 24, out_specs, scratch
        )(*low, *high, pair, *moved, columns, hidden_columns, w_ins[block_no], out_weight)
        if last:
            return outs[0]
        near, pair, duo, far = outs[0], outs[1], outs[2], outs[3:]


def solution(mesh):
    return jax.shard_map(
        shards,
        mesh=mesh,
        in_specs=(P("batch", "seq"), P(), P(), P(), P(), P()),
        out_specs=P("batch", "seq"),
        check_vma=False,
    )
```

```python
import functools

import jax
import jax.numpy as jnp
from jax import lax
from jax.experimental import pallas as pl
from jax.experimental.pallas import tpu as pltpu
from jax.sharding import PartitionSpec as P

TRACK_CH = 16
TRACKS = 19
BLOCKS = 2
LANES = 128
NEAR_TILE = 1024
TILE = 2048
LAST_TILE = 1024
COST = 1
GELU_A = 0.7978845608028654
ALPHA = (GELU_A * 0.044715) ** (1.0 / 3.0)
GELU_C = GELU_A / ALPHA
F32, BF16 = jnp.float32, jnp.bfloat16
VMEM = pl.BlockSpec(memory_space=pltpu.VMEM)


def shifted(value, axis, steps):
    count = lax.axis_size(axis)
    pairs = [(source, (source + steps) % count) for source in range(count)]
    return lax.ppermute(value, axis, pairs)


def after(value, *others):
    return lax.optimization_barrier((value, *others))[0]


def short_tracks(local_rows):
    count = 0
    while count + 1 < TRACKS and 2**count < local_rows:
        count = count + 1
    return count


def pack_halo(track, store, local_rows, short_count):
    lane = lax.broadcasted_iota(jnp.int32, (TRACK_CH, LANES), 1)
    packed = jnp.zeros((TRACK_CH, LANES), F32)
    for slot in range(short_count):
        offset = 2**slot
        if offset < LANES:
            last = track(1 + slot, local_rows - LANES, local_rows).astype(F32)
            moved = pltpu.roll(last, (2 * offset - 1) % LANES, 1)
            inside = (lane >= offset - 1) & (lane < 2 * offset - 1)
            packed = jnp.where(inside, moved, packed)
        else:
            store(offset, 2 * offset, track(1 + slot, local_rows - offset, local_rows))
    store(0, LANES, packed.astype(BF16))


def rotated_piece(track, halo, slot, begin, end):
    offset = 2**slot
    if offset < LANES:
        if begin == 0:
            packed = halo(0, LANES).astype(F32)
            before = pltpu.roll(packed, (LANES + 1 - 2 * offset) % LANES, 1)
            window = jnp.concatenate([before, track(1 + slot, 0, end).astype(F32)], 1)
        else:
            window = track(1 + slot, begin - LANES, end).astype(F32)
        return pltpu.roll(window, offset, 1)[:, LANES:].astype(BF16)
    parts = []
    if begin < offset:
        parts.append(halo(offset + begin, offset + min(end, offset)))
    if end > offset:
        parts.append(track(1 + slot, max(begin, offset) - offset, end - offset))
    return parts[0] if len(parts) == 1 else jnp.concatenate(parts, 1)


def first_kernel(short_count, tokens, *refs):
    pair, far = refs[0], refs[1:6]
    tail, sems = refs[6], refs[7:]
    near_rows, half_rows = tail.shape
    local_rows = pair.shape[1]
    base = local_rows - half_rows
    copies = [pltpu.make_async_copy(tokens.at[:near_rows, base:], tail, sems[0])]
    for at, target in enumerate([pair.at[TRACK_CH:, :], *far]):
        top = near_rows + at * TRACK_CH
        copies.append(
            pltpu.make_async_copy(tokens.at[top : top + TRACK_CH, :], target, sems[1 + at])
        )
    for copy in copies:
        copy.start()
    copies[0].wait()

    def track(t, begin, end):
        return tail[t * TRACK_CH : (t + 1) * TRACK_CH, begin - base : end - base]

    def store(begin, end, value):
        pair[:TRACK_CH, begin:end] = value

    pack_halo(track, store, local_rows, short_count)
    for copy in copies[1:]:
        copy.wait()


def start_kernel(short_count, half_rows, transposed, bias, gain, last_bias, tokens, *refs):
    outs, high, made, sems = refs[:4], refs[4:7], refs[7:11], refs[11:15]
    loaded, load_sems = refs[15:17], refs[17:19]
    depth, hidden = transposed.shape[1:]
    loads, copies = [], []
    for block_no in range(BLOCKS):
        loads.append(pltpu.make_async_copy(transposed.at[block_no], loaded[block_no], load_sems[block_no]))
        loads[-1].start()

    def send(at):
        copies.append(pltpu.make_async_copy(made[at], outs[at], sems[at]))
        copies[-1].start()

    columns = [gain[...], last_bias[...], jnp.zeros((8 - 2 * BLOCKS, depth), F32)]
    made[2][...] = jnp.transpose(jnp.concatenate(columns, 0))
    made[3][...] = jnp.transpose(jnp.concatenate([bias[...], jnp.zeros((8 - BLOCKS, hidden), F32)], 0))
    send(2)
    send(3)
    near_rotate(short_count, half_rows, tokens, None, high[0], high[1])
    for block_no in range(BLOCKS):
        loads[block_no].wait()
        made[block_no][...] = jnp.transpose(loaded[block_no][...])
        send(block_no)
        if block_no == 0:
            near_product(0, made[2], made[0], high[0], high[2])
    for copy in copies:
        copy.wait()


def near_rotate(short_count, first, near, halo_in, rotated, squares):
    width = rotated.shape[1]

    def track(t, begin, end):
        return near[t * TRACK_CH : (t + 1) * TRACK_CH, begin:end]

    def halo(begin, end):
        return halo_in[:TRACK_CH, begin:end]

    for at in range(0, width, NEAR_TILE):
        begin, end = first + at, first + at + NEAR_TILE
        total = jnp.zeros((8, NEAR_TILE), F32)
        for t in range(1 + short_count):
            piece = track(0, begin, end) if t == 0 else rotated_piece(track, halo, t - 1, begin, end)
            rotated[t * TRACK_CH : (t + 1) * TRACK_CH, at : at + NEAR_TILE] = piece
            piece = piece.astype(F32)
            total = total + (piece[:8] * piece[:8] + piece[8:] * piece[8:])
        squares[:, at : at + NEAR_TILE] = total


def near_product(block_no, columns, w_in, rotated, partial):
    near_rows, width = rotated.shape
    gain = columns[:near_rows, block_no : block_no + 1]
    for at in range(0, width, NEAR_TILE):
        here = slice(at, at + NEAR_TILE)
        scaled = (rotated[:, here].astype(F32) * gain).astype(BF16)
        partial[:, here] = jnp.dot(w_in[:, :near_rows], scaled, preferred_element_type=F32).astype(BF16)


def near_kernel(short_count, block_no, first, near, columns, w_in, *refs):
    rotated, squares, partial = refs[-3:]
    near_rotate(short_count, first, near, refs[0], rotated, squares)
    near_product(block_no, columns, w_in, rotated, partial)


def main_kernel(short_count, block_no, last, *refs):
    nears, pair, far = refs[:6], refs[6], refs[7:12]
    (columns, hidden_columns, w_in, w_out), outs = refs[12:16], refs[16:]
    copies = []
    near_rows, half_rows = nears[0].shape
    local_rows = pair.shape[1]
    width = near_rows + (1 + len(far)) * TRACK_CH
    gain = columns[near_rows:, block_no : block_no + 1]
    b_out = columns[:, BLOCKS + block_no : BLOCKS + block_no + 1]
    b_in = hidden_columns[:, block_no : block_no + 1] * ALPHA
    tile = LAST_TILE if last else TILE
    for begin in range(0, local_rows, tile):
        end = begin + tile
        rotated, squares, partial = nears[:3] if begin < half_rows else nears[3:]
        here = slice(begin % half_rows, begin % half_rows + tile)
        parts = [pair[TRACK_CH:, begin:end].astype(F32)]
        parts += [ref[:TRACK_CH, begin:end].astype(F32) for ref in far]
        total = squares[:, here]
        for part in parts:
            total = total + (part[:8] * part[:8] + part[8:] * part[8:])
        scale = ALPHA * lax.rsqrt(jnp.sum(total, axis=0, keepdims=True) * (1.0 / width) + 1e-06)
        far_part = jnp.concatenate(parts, 0)
        pre = jnp.dot(w_in[:, near_rows:], (far_part * gain).astype(BF16), preferred_element_type=F32)
        pre = (partial[:, here].astype(F32) + pre) * scale + b_in
        inner = pre * (GELU_C + pre * pre)
        active = (pre * (1.0 + jnp.tanh(inner))).astype(BF16)
        out = jnp.dot(w_out[block_no], active, preferred_element_type=F32) * (0.5 / ALPHA) + b_out
        near_out = (rotated[:, here].astype(F32) + out[:near_rows]).astype(BF16)
        far_out = (far_part + out[near_rows:]).astype(BF16)
        if last:
            made = outs[1]
            made[:near_rows, begin:end] = near_out
            made[near_rows:, begin:end] = far_out
            copy = pltpu.make_async_copy(
                made.at[:, begin:end], outs[0].at[:, begin:end], outs[2 + len(copies)]
            )
            copy.start()
            copies.append(copy)
        else:
            outs[0][:, begin:end] = near_out
            outs[1][TRACK_CH:, begin:end] = far_out[:TRACK_CH]
            for at in range(len(far)):
                outs[2 + at][:, begin:end] = far_out[(1 + at) * TRACK_CH : (2 + at) * TRACK_CH]
    for copy in copies:
        copy.wait()
    if not last:

        def track(t, begin, end):
            return outs[0][t * TRACK_CH : (t + 1) * TRACK_CH, begin:end]

        def store(begin, end, value):
            outs[1][:TRACK_CH, begin:end] = value

        pack_halo(track, store, local_rows, short_count)


def call(kernel, out_shape, in_specs, name, limit, out_specs=None, scratch=()):
    return pl.pallas_call(
        kernel,
        out_shape=out_shape,
        in_specs=in_specs,
        out_specs=out_specs or [VMEM] * len(out_shape),
        scratch_shapes=scratch,
        compiler_params=pltpu.CompilerParams(vmem_limit_bytes=limit << 20),
        cost_estimate=pl.CostEstimate(flops=COST, transcendentals=0, bytes_accessed=COST),
        name=name,
    )


def permuted(value, moves):
    return lax.ppermute(value, "seq", moves)


def routes():
    first, second = [], []
    for y in range(4):
        for z in range(8):
            for x in range(2):
                source = (y * 8 + z) * 2 + x
                middle = (((y + z // 4) % 4) * 8 + (z - 2) % 8) * 2 + x
                first.append((source, middle))
                second.append((middle, (source + 8) % 64))
    return first, second


def exchange(pair, far, fill):
    two, four, eight, sixteen, thirty_two = far
    to_middle, from_middle = routes()
    eight = permuted(eight, to_middle)
    pair = shifted(pair, "seq", 1)
    back = shifted(thirty_two, "seq", -16)
    four = shifted(four, "seq", 4)
    two = shifted(two, "seq", 2)
    eight = permuted(after(eight, *fill), from_middle)
    back = shifted(back, "seq", -16)
    sixteen = shifted(after(sixteen, two), "seq", 16)
    return pair, [two, four, eight, sixteen, back]


def shards(tokens, norm_gain, in_weight, in_bias, out_weight, out_bias):
    width, local_rows = tokens.shape
    half_rows = local_rows // 2
    hidden = in_weight.shape[1]
    short_count = short_tracks(local_rows)
    far_count = TRACKS - 2 - short_count
    near_rows = (1 + short_count) * TRACK_CH
    one = jax.ShapeDtypeStruct((TRACK_CH, local_rows), BF16)
    two = jax.ShapeDtypeStruct((2 * TRACK_CH, local_rows), BF16)
    near_shape = jax.ShapeDtypeStruct((near_rows, local_rows), BF16)
    half_shapes = [
        jax.ShapeDtypeStruct((near_rows, half_rows), BF16),
        jax.ShapeDtypeStruct((8, half_rows), F32),
        jax.ShapeDtypeStruct((hidden, half_rows), BF16),
    ]
    pair, *far = pl.pallas_call(
        functools.partial(first_kernel, short_count),
        out_shape=[two] + [one] * far_count,
        in_specs=[pl.BlockSpec(memory_space=pl.ANY)],
        out_specs=[VMEM] * (1 + far_count),
        scratch_shapes=[pltpu.VMEM((near_rows, local_rows // 2), BF16)]
        + [pltpu.SemaphoreType.DMA] * (2 + far_count),
        name="first",
    )(tokens)
    made = [((hidden, width), BF16)] * BLOCKS + [((width, 8), F32), ((hidden, 8), F32)]
    *w_ins, columns, hidden_columns, rotated, squares, partial = pl.pallas_call(
        functools.partial(start_kernel, short_count, half_rows),
        out_shape=[jax.ShapeDtypeStruct(*entry) for entry in made] + half_shapes,
        in_specs=[pl.BlockSpec(memory_space=pltpu.HBM)] + [VMEM] * 4,
        out_specs=[pl.BlockSpec(memory_space=pltpu.HBM)] * 4 + [VMEM] * 3,
        scratch_shapes=[pltpu.VMEM(*entry) for entry in made]
        + [pltpu.SemaphoreType.DMA] * 4
        + [pltpu.VMEM((width, hidden), BF16)] * BLOCKS
        + [pltpu.SemaphoreType.DMA] * BLOCKS,
        compiler_params=pltpu.CompilerParams(vmem_limit_bytes=16 << 20),
        name="start",
    )(pltpu.with_memory_space_constraint(jnp.swapaxes(in_weight, 1, 2), pltpu.HBM), in_bias, norm_gain, out_bias, tokens)
    high = [rotated, squares, partial]
    near = tokens
    for block_no in range(BLOCKS):
        last = block_no == BLOCKS - 1
        if block_no:
            high = call(
                functools.partial(near_kernel, short_count, block_no, half_rows), half_shapes, [VMEM] * 3, "high", 8
            )(near, columns, w_ins[block_no])
        pair, moved = exchange(pair, far, [high[1]])
        low = call(functools.partial(near_kernel, short_count, block_no, 0), half_shapes, [VMEM] * 4, "low", 8)(
            near, columns, w_ins[block_no], pair
        )
        out_shape = [jax.ShapeDtypeStruct((width, local_rows), BF16)]
        if not last:
            out_shape = [near_shape, two] + [one] * far_count
        out_specs, scratch = [VMEM] * len(out_shape), []
        if last:
            out_specs = [pl.BlockSpec(memory_space=pltpu.HBM)]
            scratch = [pltpu.VMEM((width, local_rows), BF16)] + [pltpu.SemaphoreType.DMA] * (local_rows // LAST_TILE)
        outs = call(
            functools.partial(main_kernel, short_count, block_no, last), out_shape, [VMEM] * 16, "main", 24, out_specs, scratch
        )(*low, *high, pair, *moved, columns, hidden_columns, w_ins[block_no], out_weight)
        if last:
            return outs[0]
        near, pair, far = outs[0], outs[1], outs[2:]


def solution(mesh):
    return jax.shard_map(
        shards,
        mesh=mesh,
        in_specs=(P("batch", "seq"), P(), P(), P(), P(), P()),
        out_specs=P("batch", "seq"),
        check_vma=False,
    )
```
